512 devices in a mesh: seq: 64 (over z, y), head: 8 (over x, core).
Axes of the slice: x: 4, y: 4, z: 16, core: 2. Of those that a mesh axis runs over, the one named last changes fastest.
Arguments:
- queries: bfloat16 [65536, 2048], P('seq', 'head'), may hold values from -6 to 6
- keys: bfloat16 [65536, 2048], P('seq', 'head'), may hold values from -6 to 6
- values: bfloat16 [65536, 2048], P('seq', 'head'), may hold values from -6 to 6
- offsets: int32 [16, 3], P('head'), may hold values from 0 to 63, as said below
- w_out: bfloat16 [2048, 2048], P('head'), may hold values from -0.1875 to 0.1875
Outputs:
- projected: bfloat16 [65536, 2048], P('seq', 'head')
The draws below stay inside these ranges and needn't reach their ends.
Inputs may be any that keep to these rules, and one draw needn't show every extreme that they name: offsets[h, 0] is below 4, offsets[h, 1] below 16, offsets[h, 2] below 64.
All inputs are finite; a program needn't handle non-finite values.
Results may differ from the reference program's by a relative error of at most 0.017.
Values may be sent and summed in bfloat16 or wider, within the bound.
No kernel may reach another device: no remote copies, remote signals or barrier semaphores. Data moves between devices by JAX's collectives and lax.ppermute only.
A program may use at most 64 MiB of HBM per device.

```python
import jax
import jax.numpy as jnp
from jax import lax

HEADS = 16
HEAD_DIM = 128
D = 2048
TOK_DEV = 1024
TOKENS = 65536
WHOLE_DILATION = 64
N_HEAD = 8


def draw_queries(key, part):
    base = jnp.clip(jax.random.normal(jax.random.fold_in(key, 11), (TOKENS, D), jnp.float32), -6.0, 6.0)
    return base.astype(jnp.bfloat16)


def draw_keys(key, part):
    base = jnp.clip(jax.random.normal(jax.random.fold_in(key, 17), (TOKENS, D), jnp.float32), -6.0, 6.0)
    return base.astype(jnp.bfloat16)


def draw_offsets(key, part):
    level_limits = jnp.array([4, 16, WHOLE_DILATION], jnp.int32)
    sampled_rows = jax.random.randint(jax.random.fold_in(key, 5), (HEADS, 3), 0, level_limits[None, :])
    low_head = jax.random.randint(jax.random.fold_in(key, 23), (), 0, HEADS)
    upper_head = jax.random.randint(jax.random.fold_in(key, 29), (), 0, HEADS)
    head_numbers = jnp.arange(HEADS)
    first = jnp.where(head_numbers == low_head, 0, sampled_rows[:, 0])
    final_entry = jnp.where(head_numbers == upper_head, WHOLE_DILATION - 1, sampled_rows[:, 2])
    return jnp.stack([first, sampled_rows[:, 1], final_entry], axis=1).astype(jnp.int32)


def with_spikes(values, stream_key, source, target, parts, factor):
    def block_of(dim):
        return (jnp.arange(values.shape[dim]) // (values.shape[dim] // parts)).reshape((-1,) + (1,) * (values.ndim - 1 - dim))

    one_side = jax.random.permutation(stream_key, parts)[block_of(target)]
    other_side = (block_of(target) + parts // 2) % parts
    return jnp.where((block_of(source) == one_side) | (block_of(source) == other_side), factor * values, values)


def block_levels(own_key, dims, cuts, smallest, largest):
    gain, own = 1.0, jax.random.fold_in(own_key, 6)
    for dim, blocks in cuts:
        heights = jnp.exp(jax.random.uniform(jax.random.fold_in(own, dim), (blocks,), jnp.float32, smallest / len(cuts), largest / len(cuts)))
        gain = gain * jnp.repeat(heights, dims[dim] // blocks).reshape([-1 if axis == dim else 1 for axis in range(len(dims))])
    return gain


def noise(rng, extent, width, limit, pieces=(), held_as=jnp.bfloat16):
    factor_of = block_levels(rng, extent, pieces, -0.22, 0.18) if pieces else 1.0
    values = jax.random.normal(rng, extent, jnp.float32) * width * factor_of
    return jnp.minimum(jnp.maximum(values, -limit), limit).astype(held_as)


def noise_with(rng, extent, deviation, reach, pieces, heavy, held_as=jnp.bfloat16):
    values = deviation * jax.random.normal(rng, extent, jnp.float32)
    if pieces:
        values = values * block_levels(rng, extent, pieces, -0.22, 0.18)
    return jnp.clip(with_spikes(values, jax.random.fold_in(rng, 3), *heavy), -reach, reach).astype(held_as)


def setup_inputs(seed: int = 0) -> dict:
    arg_keys = jax.random.split(jax.random.key(seed), 6)
    queries = draw_queries(jax.random.fold_in(arg_keys[5], 71), 0)
    keys = draw_keys(jax.random.fold_in(arg_keys[5], 71), 0)
    values = noise(arg_keys[2], (TOKENS, D), 1.0, 6.0, ((0, 64), (1, 8)))
    offsets = draw_offsets(jax.random.fold_in(arg_keys[5], 71), 0)
    w_out = noise_with(arg_keys[4], (D, D), D ** -0.5, 0.1875, ((0, 8),), (0, 1, 8, 2.0))
    return dict(queries=queries, keys=keys, values=values, offsets=offsets, w_out=w_out)


def choose_rows(source, dilation_step, level_offsets):
    count = source.shape[0] // dilation_step
    grid = source.reshape(count, dilation_step, HEADS, HEAD_DIM)
    index = jnp.broadcast_to(level_offsets.reshape(1, 1, HEADS, 1).astype(jnp.int32), (count, 1, HEADS, HEAD_DIM))
    return jnp.take_along_axis(grid, index, axis=1)[:, 0]


def segment_attend(blocks):
    query_block, key_block, value_block = blocks
    scores = jnp.einsum("qhd,khd->hqk", query_block.astype(jnp.float32), key_block.astype(jnp.float32)) * (HEAD_DIM ** -0.5)
    query_index = lax.broadcasted_iota(jnp.int32, (TOK_DEV, TOK_DEV), 0)
    key_index = lax.broadcasted_iota(jnp.int32, (TOK_DEV, TOK_DEV), 1)
    scores = jnp.where((key_index <= query_index)[None], scores, jnp.float32(-1e30))
    maxima = jnp.max(scores, axis=-1)
    weights = jnp.exp(scores - maxima[..., None])
    totals = jnp.sum(weights, axis=-1)
    rounded = lax.optimization_barrier(weights.astype(jnp.bfloat16))
    summed = jnp.einsum("hqk,khd->qhd", rounded.astype(jnp.float32), value_block.astype(jnp.float32))
    return summed, maxima.T, totals.T


def level_terms(query_grid, key_grid, value_grid, dilation_step, level_offsets):
    count = TOKENS // dilation_step
    chosen_q = choose_rows(query_grid, dilation_step, level_offsets).reshape(count // TOK_DEV, TOK_DEV, HEADS, HEAD_DIM)
    chosen_k = choose_rows(key_grid, dilation_step, level_offsets).reshape(count // TOK_DEV, TOK_DEV, HEADS, HEAD_DIM)
    chosen_v = choose_rows(value_grid, dilation_step, level_offsets).reshape(count // TOK_DEV, TOK_DEV, HEADS, HEAD_DIM)
    summed, maxima, totals = lax.map(segment_attend, (chosen_q, chosen_k, chosen_v))
    summed = summed.reshape(count, HEADS, HEAD_DIM)
    maxima = maxima.reshape(count, HEADS)
    totals = totals.reshape(count, HEADS)
    picked = lax.broadcasted_iota(jnp.int32, (1, dilation_step, HEADS), 1) == level_offsets.reshape(1, 1, HEADS).astype(jnp.int32)
    summed = jnp.where(picked[..., None], summed[:, None], jnp.float32(0.0)).reshape(TOKENS, HEADS, HEAD_DIM)
    maxima = jnp.where(picked, maxima[:, None], jnp.float32(-1e30)).reshape(TOKENS, HEADS)
    totals = jnp.where(picked, totals[:, None], jnp.float32(0.0)).reshape(TOKENS, HEADS)
    return maxima, summed, totals


def combine(run_state, terms):
    old_top, old_sum, old_total = run_state
    level_max, level_sum, level_total = terms
    new_top = jnp.maximum(old_top, level_max)
    keep_old = jnp.exp(old_top - new_top)
    keep_new = jnp.exp(level_max - new_top)
    return new_top, old_sum * keep_old[..., None] + level_sum * keep_new[..., None], old_total * keep_old + level_total * keep_new


def reference(queries, keys, values, offsets, w_out):
    query_grid = queries.reshape(TOKENS, HEADS, HEAD_DIM)
    key_grid = keys.reshape(TOKENS, HEADS, HEAD_DIM)
    value_grid = values.reshape(TOKENS, HEADS, HEAD_DIM)
    zero_offsets = jnp.zeros((HEADS,), jnp.int32)
    run_state = level_terms(query_grid, key_grid, value_grid, 1, zero_offsets)
    for column_slot, dilation_step in ((0, 4), (1, 16), (2, WHOLE_DILATION)):
        terms = level_terms(query_grid, key_grid, value_grid, dilation_step, offsets[:, column_slot])
        run_state = combine(run_state, terms)
    attention = (run_state[1] / run_state[2][..., None]).astype(jnp.bfloat16).reshape(TOKENS, D)
    columns = D // N_HEAD
    result = jnp.zeros((TOKENS, D), jnp.float32)
    for group in range(N_HEAD):
        partial_term = jnp.dot(attention[:, group * columns:(group + 1) * columns], w_out[group * columns:(group + 1) * columns], preferred_element_type=jnp.float32)
        partial_term = lax.optimization_barrier(partial_term.astype(jnp.bfloat16))
        result = result + partial_term.astype(jnp.float32)
    return result.astype(jnp.bfloat16)
```

```python
import math

import jax
import jax.numpy as jnp
from jax import lax
from jax.experimental import pallas as pl
from jax.experimental.pallas import tpu as pltpu
from jax.sharding import PartitionSpec as P

HEAD_DIM = 128
SCALE = HEAD_DIM ** (-0.5)
SCALE2 = SCALE * math.log2(math.e)
NEG = -1e30
F32 = jnp.float32
BF16 = jnp.bfloat16
STEPS = (4, 16, 64)
VMEM = pl.BlockSpec(memory_space=pltpu.VMEM)
SMEM = pl.BlockSpec(memory_space=pltpu.SMEM)
PARAMS = pltpu.CompilerParams(vmem_limit_bytes=48 << 20)


def half(head):
    return slice(head * HEAD_DIM, (head + 1) * HEAD_DIM)


def rows_of(offset, total, step):
    return pl.ds(offset, total // step, stride=step)


def call(kernel, out, specs, scratch=()):
    return pl.pallas_call(
        kernel,
        out_shape=out,
        in_specs=specs,
        out_specs=jax.tree.map(lambda _: VMEM, out),
        scratch_shapes=scratch,
        compiler_params=PARAMS,
    )


def shape(dims, dtype):
    return jax.ShapeDtypeStruct(dims, dtype)


def pick_kernel(off, q, k, v, near, middle, whole, own_q, wide):
    rows = q.shape[0]
    for head in range(2):
        for slot, source in enumerate((q, k, v)):
            wide[slot] = source[:, half(head)].astype(F32)

        def pick(slot, level):
            return wide[slot, rows_of(off[head, level], rows, STEPS[level]), :].astype(BF16)

        count = [rows // step for step in STEPS]
        own_q[:, half(head)] = pick(0, 0)
        parts = (pick(1, 0), pick(2, 0), pick(0, 1), pick(0, 2))
        for target in range(near.shape[0]):
            at = 0
            for part in parts:
                near[target, at : at + part.shape[0], half(head)] = part
                at += part.shape[0]
        for level, out in ((1, middle), (2, whole)):
            keys, values = pick(1, level), pick(2, level)
            for target in range(out.shape[0]):
                out[target, : count[level], half(head)] = keys
                out[target, count[level] :, half(head)] = values


def local_kernel(off, q, k, v, early, mixed, logs):
    rows = q.shape[0]
    block = 256
    for head in range(2):
        for first in range(0, rows, block):
            last = first + block
            scores = lax.dot_general(
                q[first:last, half(head)], k[:last, half(head)], (((1,), (1,)), ((), ())), preferred_element_type=F32
            )
            query = first + lax.broadcasted_iota(jnp.int32, scores.shape, 0)
            key = lax.broadcasted_iota(jnp.int32, scores.shape, 1)
            scores = jnp.where(key <= query, scores, NEG)
            top = jnp.max(scores, axis=-1, keepdims=True)
            weights = jnp.exp2((scores - top) * SCALE2)
            total = jnp.sum(weights, axis=-1, keepdims=True)
            out = jnp.dot(weights.astype(BF16), v[:last, half(head)], preferred_element_type=F32) / total
            mixed[head, first:last, :] = out
            logs[head, first:last, :] = jnp.broadcast_to(top * SCALE + jnp.log(total), out.shape)
            for target in range(early.shape[0]):
                early[target, first:last, half(head)] = out.astype(BF16)
        line = lax.broadcasted_iota(jnp.int32, (16, HEAD_DIM), 0)
        marks = jnp.where(line == 0, off[head, 0], jnp.where(line == 1, off[head, 1], off[head, 2]))
        for target in range(early.shape[0]):
            early[target, rows:, half(head)] = marks.astype(F32).astype(BF16)


def near_kernel(own_q, near, mixed, logs):
    count = own_q.shape[0]
    place = lax.rem(lax.axis_index("seq"), near.shape[0]) * count
    for head in range(2):
        keys = near[:, :count, half(head)].reshape(-1, HEAD_DIM)
        values = near[:, count : 2 * count, half(head)].reshape(-1, HEAD_DIM)
        scores = lax.dot_general(own_q[:, half(head)], keys, (((1,), (1,)), ((), ())), preferred_element_type=F32)
        query = place + lax.broadcasted_iota(jnp.int32, scores.shape, 0)
        key = lax.broadcasted_iota(jnp.int32, scores.shape, 1)
        scores = jnp.where(key <= query, scores, NEG)
        top = jnp.max(scores, axis=-1, keepdims=True)
        weights = jnp.exp2((scores - top) * SCALE2)
        total = jnp.sum(weights, axis=-1, keepdims=True)
        out = jnp.dot(weights.astype(BF16), values, preferred_element_type=F32) / total
        mixed[head] = out
        logs[head] = jnp.broadcast_to(top * SCALE + jnp.log(total), out.shape)


def far_kernel(near, middle, whole, back):
    across = near.shape[0]
    seq = lax.axis_index("seq")
    column, line = lax.rem(seq, across), lax.div(seq, across)
    skip = 512
    at = 0
    for level, source in ((1, middle), (2, whole)):
        blocks = source.shape[0]
        count = source.shape[1] // 2
        place = lax.rem(line, blocks) if level == 1 else line
        logs = []
        for head in range(2):
            queries = near[:, skip + at : skip + at + count, half(head)].reshape(-1, HEAD_DIM)
            keys = source[:, :count, half(head)].reshape(-1, HEAD_DIM)
            values = source[:, count:, half(head)].reshape(-1, HEAD_DIM)
            scores = lax.dot_general(queries, keys, (((1,), (1,)), ((), ())), preferred_element_type=F32)
            query = place * (across * count) + lax.broadcasted_iota(jnp.int32, scores.shape, 0)
            key = lax.broadcasted_iota(jnp.int32, scores.shape, 1)
            key = (lax.div(key, count) * across + column) * count + lax.rem(key, count)
            kept = key <= query
            scores = jnp.where(kept, scores, NEG)
            top = jnp.max(scores, axis=-1, keepdims=True)
            weights = jnp.where(kept, jnp.exp2((scores - top) * SCALE2), 0.0)
            total = jnp.sum(weights, axis=-1, keepdims=True)
            some = total > 0.0
            safe = jnp.where(some, total, 1.0)
            out = jnp.dot(weights.astype(BF16), values, preferred_element_type=F32) / safe
            logs.append(jnp.where(some, top * SCALE + jnp.log(safe), NEG))
            back[:, at : at + count, half(head)] = out.reshape(across, count, HEAD_DIM)
        lane = lax.broadcasted_iota(jnp.int32, (across * count, HEAD_DIM), 1)
        both = jnp.where(lane < HEAD_DIM // 2, logs[0], logs[1])
        back[:, at : at + count, 2 * HEAD_DIM :] = both.reshape(across, count, HEAD_DIM)
        at += count


def merge(parts):
    top = parts[0][1]
    for _, log in parts[1:]:
        top = jnp.maximum(top, log)
    total, out = 0.0, 0.0
    for value, log in parts:
        share = jnp.exp(log - top)
        total = total + share
        out = out + share * value
    return out / total, top + jnp.log(total)


def merge_kernel(off, mixed, logs, near_mixed, near_logs, back, late, run, run_logs):
    rows = mixed.shape[1]
    for head in range(2):
        run[head] = mixed[head]
        run_logs[head] = logs[head]
        at = 0
        for level, step in enumerate(STEPS):
            count = rows // step
            where = rows_of(off[head, level], rows, step)
            if level == 0:
                new = (near_mixed[head], near_logs[head])
            else:
                parts = []
                for source in range(back.shape[0]):
                    lane = 2 * HEAD_DIM + head * (HEAD_DIM // 2)
                    log = back[source, at : at + count, lane : lane + 1]
                    parts.append(
                        (back[source, at : at + count, half(head)], jnp.broadcast_to(log, (count, HEAD_DIM)))
                    )
                new = merge(parts)
                at += count
            out, log = merge([(run[head, where, :], run_logs[head, where, :]), new])
            run[head, where, :] = out
            run_logs[head, where, :] = log
        at = 0
        for level, step in enumerate(STEPS):
            count = rows // step
            final = run[head, rows_of(off[head, level], rows, step), :].astype(BF16)
            for target in range(late.shape[0]):
                late[target, at : at + count, half(head)] = final
            at += count


def project_kernel(marks, early, late, weight, send, keep, wide, whole):
    rows = send.shape[0]
    for group in range(early.shape[0]):
        for head in range(2):
            slot = 2 * group + head
            wide[slot] = early[group, :rows, half(head)].astype(F32)
            at = 0
            for level, step in enumerate(STEPS):
                count = rows // step
                wide[slot, rows_of(marks[group, level, head], rows, step), :] = late[
                    group, at : at + count, half(head)
                ].astype(F32)
                at += count
            whole[:, half(slot)] = wide[slot].astype(BF16)
    core = lax.rem(lax.axis_index("head"), 2)
    width = keep.shape[1]

    def product(which):
        columns = pl.ds(pl.multiple_of(which * width, width), width)
        return jnp.dot(whole[...], weight[:, columns], preferred_element_type=F32)

    send[...] = product(1 - core).astype(BF16)
    keep[...] = product(core)


def shards(queries, keys, values, offsets, w_out):
    rows, width = queries.shape
    spread, heads = lax.axis_size("seq"), lax.axis_size("head")
    across, cores = 4, 2
    lines, chips = spread // across, heads // cores
    along_y = [[line * across + y for y in range(across)] for line in range(lines)]
    along_z = [[line * across + y for line in range(lines)] for y in range(across)]
    blocks_z = [[(4 * b + line) * across + y for line in range(4)] for b in range(lines // 4) for y in range(across)]
    along_x = [[chip * cores + core for chip in range(chips)] for core in range(cores)]

    def swap(value, axis, groups):
        return lax.all_to_all(value, axis, 0, 0, axis_index_groups=groups)

    count = [rows // step for step in STEPS]
    near_rows = 2 * count[0] + count[1] + count[2]
    near, middle, whole, own_q = call(
        pick_kernel,
        (
            shape((across, near_rows, width), BF16),
            shape((4, 2 * count[1], width), BF16),
            shape((lines, 2 * count[2], width), BF16),
            shape((count[0], width), BF16),
        ),
        [SMEM, VMEM, VMEM, VMEM],
        [pltpu.VMEM((3, rows, HEAD_DIM), F32)],
    )(offsets, queries, keys, values)
    whole = swap(whole, "seq", along_z)
    near = swap(near, "seq", along_y)
    middle = swap(middle, "seq", blocks_z)
    weight = w_out.reshape(width, chips, cores * width).transpose(1, 0, 2)
    weight = swap(weight, "head", along_x).reshape(chips * width, cores * width)
    early, mixed, logs = call(
        local_kernel,
        (
            shape((chips, rows + 16, width), BF16),
            shape((2, rows, HEAD_DIM), F32),
            shape((2, rows, HEAD_DIM), F32),
        ),
        [SMEM, VMEM, VMEM, VMEM],
    )(offsets, queries, keys, values)
    early = swap(early, "head", along_x)
    marks = early[:, rows : rows + 3, ::HEAD_DIM].astype(jnp.int32)
    near_mixed, near_logs = call(
        near_kernel,
        (shape((2, count[0], HEAD_DIM), F32), shape((2, count[0], HEAD_DIM), F32)),
        [VMEM, VMEM],
    )(own_q, near)
    back = call(
        far_kernel,
        shape((across, count[1] + count[2], 3 * HEAD_DIM), F32),
        [VMEM, VMEM, VMEM],
    )(near, middle, whole)
    back = swap(back, "seq", along_y)
    late = call(
        merge_kernel,
        shape((chips, sum(count), width), BF16),
        [SMEM] + [VMEM] * 5,
        [pltpu.VMEM((2, rows, HEAD_DIM), F32), pltpu.VMEM((2, rows, HEAD_DIM), F32)],
    )(offsets, mixed, logs, near_mixed, near_logs, back)
    late = swap(late, "head", along_x)
    send, keep = call(
        project_kernel,
        (shape((rows, width), BF16), shape((rows, width), F32)),
        [SMEM, VMEM, VMEM, VMEM],
        [pltpu.VMEM((2 * chips, rows, HEAD_DIM), F32), pltpu.VMEM((rows, chips * width), BF16)],
    )(marks, early, late, weight)
    other = lax.ppermute(send, "head", [(device, device ^ 1) for device in range(heads)])
    return (keep + other.astype(F32)).astype(BF16)


def solution(mesh):
    in_specs = (
        P("seq", "head"),
        P("seq", "head"),
        P("seq", "head"),
        P("head", None),
        P("head", None),
    )
    out_specs = P("seq", "head")
    return jax.shard_map(shards, mesh=mesh, in_specs=in_specs, out_specs=out_specs, check_vma=False)
```

```python
import math

import jax
import jax.numpy as jnp
from jax import lax
from jax.experimental import pallas as pl
from jax.experimental.pallas import tpu as pltpu
from jax.sharding import PartitionSpec as P

HEAD_DIM = 128
SCALE = HEAD_DIM ** (-0.5)
SCALE2 = SCALE * math.log2(math.e)
NEG = -1e30
F32 = jnp.float32
BF16 = jnp.bfloat16
STEPS = (4, 16, 64)
VMEM = pl.BlockSpec(memory_space=pltpu.VMEM)
SMEM = pl.BlockSpec(memory_space=pltpu.SMEM)
HBM = pl.BlockSpec(memory_space=pltpu.HBM)
ANY = pl.BlockSpec(memory_space=pl.ANY)
PARAMS = pltpu.CompilerParams(vmem_limit_bytes=20 << 20)


def half(head):
    return slice(head * HEAD_DIM, (head + 1) * HEAD_DIM)


def rows_of(offset, total, step):
    return pl.ds(offset, total // step, stride=step)


def call(kernel, out, in_specs, out_specs, scratch=()):
    return pl.pallas_call(
        kernel,
        out_shape=out,
        in_specs=in_specs,
        out_specs=out_specs,
        scratch_shapes=scratch,
        compiler_params=PARAMS,
    )


def shape(dims, dtype):
    return jax.ShapeDtypeStruct(dims, dtype)


def stay(value):
    return pltpu.with_memory_space_constraint(value, pltpu.HBM)


def copy(source, target, sem):
    moved = pltpu.make_async_copy(source, target, sem)
    moved.start()
    return moved


def attend(queries, keys, values, kept):
    scores = lax.dot_general(queries, keys, (((1,), (1,)), ((), ())), preferred_element_type=F32)
    scores = jnp.where(kept, scores, NEG)
    top = jnp.max(scores, axis=-1, keepdims=True)
    weights = jnp.where(kept, jnp.exp2((scores - top) * SCALE2), 0.0)
    total = jnp.sum(weights, axis=-1, keepdims=True)
    some = total > 0.0
    safe = jnp.where(some, total, 1.0)
    out = jnp.dot(weights.astype(BF16), values, preferred_element_type=F32) / safe
    return out, jnp.where(some, top * SCALE + jnp.log(safe), NEG)


def pick_kernel(off_in, q, k, v, near_out, near_z, own_q, off, raw, wide, near, pack, query, sems):
    rows = q.shape[0]
    count = [rows // step for step in STEPS]
    first = copy(off_in, off, sems.at[0])
    loads = [copy(source, raw.at[slot], sems.at[1 + slot]) for slot, source in enumerate((k, v, q))]
    moves = []
    first.wait()
    for slot in range(3):
        loads[slot].wait()
        for head in range(2):
            wide[slot, head] = raw[slot, :, half(head)].astype(F32)
            picks = [
                wide[slot, head, rows_of(off[head, level], rows, step), :].astype(BF16)
                for level, step in enumerate(STEPS)
            ]
            if slot < 2:
                near[slot * count[0] : (slot + 1) * count[0], half(head)] = picks[0]
                pack[slot * count[1] : (slot + 1) * count[1], half(head)] = picks[1]
                at = 2 * count[1] + slot * count[2]
                pack[at : at + count[2], half(head)] = picks[2]
            else:
                query[:, half(head)] = picks[0]
                at = 2 * count[0]
                near[at : at + count[1], half(head)] = picks[1]
                near[at + count[1] : at + count[1] + count[2], half(head)] = picks[2]
        if slot == 1:
            moves = [copy(pack, near_z, sems.at[4])]
    moves.append(copy(query, own_q, sems.at[8]))
    moves += [copy(near, near_out.at[target], sems.at[9 + target]) for target in range(4)]
    for moved in moves:
        moved.wait()


def relay_kernel(z0, z1, z2, z3, _1, _2, far_z, part, sems):
    line = lax.rem(lax.div(lax.axis_index("seq"), 4), 4)
    loads = [
        copy(z.at[pl.ds(128, 32), :], part.at[lax.rem(line + 4 - shift, 4)], sems.at[shift])
        for shift, z in enumerate((z0, z1, z2, z3))
    ]
    for moved in loads:
        moved.wait()
    moves = [copy(part, far_z.at[target], sems.at[4 + target]) for target in range(far_z.shape[0])]
    for moved in moves:
        moved.wait()


def local_kernel(off_in, q, k, v, w, own, out1, out2, out3, mixed, logs, off, raw, wide, early, some, some_logs, held, sems):
    chip = lax.div(lax.axis_index("head"), 2)
    width = q.shape[1]
    moves = []
    column = copy(w, held, sems.at[16])
    rows = q.shape[0]
    block = 256
    first_copy = copy(off_in, off, sems.at[0])
    loads = [copy(source, raw.at[slot], sems.at[1 + slot]) for slot, source in enumerate((q, k, v))]
    for moved in loads:
        moved.wait()
    first_copy.wait()
    column.wait()
    for shift, out in enumerate((out1, out2, out3), 1):
        for part in range(2):
            place = pl.multiple_of((2 * lax.rem(chip + shift, 4) + part) * width, width)
            at = 3 * rows // 4 + 16 + part * width
            moves.append(copy(held.at[:, pl.ds(place, width)], out.at[pl.ds(at, width), :], sems.at[2 + 2 * shift + part]))
    row = lax.broadcasted_iota(jnp.int32, (block, block), 0)
    kept = lax.broadcasted_iota(jnp.int32, (block, block), 1) <= row
    for head in range(2):
        for first in range(0, rows, block):
            last = first + block
            query = raw[0, first:last, half(head)]
            pieces = [(first, last)] + ([(0, first)] if first else [])
            scores = [
                lax.dot_general(
                    query, raw[1, low:high, half(head)], (((1,), (1,)), ((), ())), preferred_element_type=F32
                )
                for low, high in pieces
            ]
            scores[0] = jnp.where(kept, scores[0], NEG)
            top = jnp.max(scores[0], axis=-1, keepdims=True)
            for piece in scores[1:]:
                top = jnp.maximum(top, jnp.max(piece, axis=-1, keepdims=True))
            total, out = 0.0, 0.0
            for piece, (low, high) in zip(scores, pieces):
                weights = jnp.exp2((piece - top) * SCALE2)
                total = total + jnp.sum(weights, axis=-1, keepdims=True)
                out = out + jnp.dot(weights.astype(BF16), raw[2, low:high, half(head)], preferred_element_type=F32)
            out = out / total
            wide[0, first:last, :] = out
            wide[1, first:last, :] = jnp.broadcast_to(top * SCALE + jnp.log(total), out.shape)
        part = rows // 4
        for turn in range(3):
            where = rows_of(lax.rem(off[head, 0] + turn + 1, 4), rows, 4)
            early[turn * part : (turn + 1) * part, half(head)] = wide[0, where, :].astype(BF16)
        line = lax.broadcasted_iota(jnp.int32, (16, HEAD_DIM), 0)
        marks = jnp.where(line == 0, off[head, 0], jnp.where(line == 1, off[head, 1], off[head, 2]))
        early[3 * part :, half(head)] = marks.astype(F32).astype(BF16)
        at = 0
        for level, step in enumerate(STEPS):
            count = rows // step
            where = rows_of(off[head, level], rows, step)
            some[head, at : at + count, :] = wide[0, where, :]
            some_logs[head, at : at + count, :] = wide[1, where, :]
            at += count
    for slot, out in enumerate((own, out1, out2, out3)):
        moves.append(copy(early, out.at[pl.ds(0, 3 * rows // 4 + 16), :], sems.at[10 + slot]))
    moves += [copy(some, mixed, sems.at[14]), copy(some_logs, logs, sems.at[15])]
    for moved in moves:
        moved.wait()


def near_kernel(own_q, near_in, mixed, logs, queries, near, some, some_logs, sems):
    count = own_q.shape[0]
    loads = [copy(own_q, queries, sems.at[0]), copy(near_in.at[:, pl.ds(0, 2 * count), :], near, sems.at[3])]
    for moved in loads:
        moved.wait()
    mine = lax.rem(lax.axis_index("seq"), 4)
    for head in range(2):
        keys = near[:, :count, half(head)].reshape(-1, HEAD_DIM)
        values = near[:, count:, half(head)].reshape(-1, HEAD_DIM)
        dims = (count, 4 * count)
        query = mine * count + lax.broadcasted_iota(jnp.int32, dims, 0)
        key = lax.broadcasted_iota(jnp.int32, dims, 1)
        out, log = attend(queries[:, half(head)], keys, values, key <= query)
        some[head] = out
        some_logs[head] = jnp.broadcast_to(log, out.shape)
    moves = [copy(some, mixed, sems.at[1]), copy(some_logs, logs, sems.at[2])]
    for moved in moves:
        moved.wait()


def far_kernel(near_in, z0, z1, z2, z3, far_z, back, near, zs, hi, part, sems):
    seq = lax.axis_index("seq")
    mine, line = lax.rem(seq, 4), lax.div(seq, 4)
    loads = [copy(z.at[pl.ds(0, 128), :], zs.at[shift], sems.at[2 + shift]) for shift, z in enumerate((z0, z1, z2, z3))]
    loads.append(copy(far_z, hi, sems.at[6]))
    loads.append(copy(near_in.at[:, pl.ds(512, 80), :], near, sems.at[0]))
    for moved in loads:
        moved.wait()
    at = 0
    for level, count in ((1, 64), (2, 16)):
        place = lax.rem(line, 4) if level == 1 else line
        logs = []
        for head in range(2):
            queries = near[:, at : at + count, half(head)].reshape(-1, HEAD_DIM)
            if level == 1:
                keys = zs[:, :count, half(head)].reshape(-1, HEAD_DIM)
                values = zs[:, count:, half(head)].reshape(-1, HEAD_DIM)
            else:
                keys = hi[:, :, :count, half(head)].reshape(-1, HEAD_DIM)
                values = hi[:, :, count:, half(head)].reshape(-1, HEAD_DIM)
            dims = (4 * count, keys.shape[0])
            row = lax.broadcasted_iota(jnp.int32, dims, 0)
            query = place * 4 * count + row
            key = lax.broadcasted_iota(jnp.int32, dims, 1)
            source = lax.rem(place + 4 - lax.div(key, count), 4) if level == 1 else lax.div(key, count)
            key = (source * 4 + mine) * count + lax.rem(key, count)
            out, log = attend(queries, keys, values, key <= query)
            logs.append(log)
            part[:, at : at + count, half(head)] = out.reshape(4, count, HEAD_DIM)
        lane = lax.broadcasted_iota(jnp.int32, (4 * count, HEAD_DIM), 1)
        both = jnp.where(lane < HEAD_DIM // 2, logs[0], logs[1])
        part[:, at : at + count, 2 * HEAD_DIM :] = both.reshape(4, count, HEAD_DIM)
        at += count
    moves = [copy(part, back, sems.at[1])]
    for moved in moves:
        moved.wait()


def merge(parts):
    top = parts[0][1]
    for _, log in parts[1:]:
        top = jnp.maximum(top, log)
    total, out = 0.0, 0.0
    for value, log in parts:
        share = jnp.exp(log - top)
        total = total + share
        out = out + share * value
    return out / total, top + jnp.log(total)


def merge_kernel(off_in, m_in, l_in, nm_in, nl_in, back_in, _1, _2, _3, late, off, mixed, logs, near_mixed, near_logs, back, run, run_logs, pack, sems):
    rows = run.shape[1]
    places = ((off_in, off), (m_in, mixed), (l_in, logs), (nm_in, near_mixed), (nl_in, near_logs), (back_in, back))
    loads = [copy(source, target, sems.at[slot]) for slot, (source, target) in enumerate(places)]
    for moved in loads:
        moved.wait()
    for head in range(2):
        at = 0
        for level, step in enumerate(STEPS):
            count = rows // step
            where = rows_of(off[head, level], rows, step)
            run[head, where, :] = mixed[head, at : at + count, :]
            run_logs[head, where, :] = logs[head, at : at + count, :]
            at += count
        at = 0
        for level, step in enumerate(STEPS):
            count = rows // step
            where = rows_of(off[head, level], rows, step)
            if level == 0:
                new = (near_mixed[head], near_logs[head])
            else:
                parts = []
                for source in range(4):
                    lane = 2 * HEAD_DIM + head * (HEAD_DIM // 2)
                    log = back[source, at : at + count, lane : lane + 1]
                    parts.append(
                        (back[source, at : at + count, half(head)], jnp.broadcast_to(log, (count, HEAD_DIM)))
                    )
                new = merge(parts)
                at += count
            out, log = merge([(run[head, where, :], run_logs[head, where, :]), new])
            run[head, where, :] = out
            run_logs[head, where, :] = log
        at = 0
        for level, step in enumerate(STEPS):
            count = rows // step
            pack[at : at + count, half(head)] = run[head, rows_of(off[head, level], rows, step), :].astype(BF16)
            at += count
    moves = [copy(pack, late.at[target], sems.at[6 + target]) for target in range(4)]
    for moved in moves:
        moved.wait()


def project_kernel(marks, own, e1, e2, e3, late, w, send, keep, e0, wide, whole, weight, sems):
    rows, width = keep.shape
    part = rows // 4
    most = 3 * part
    place = lax.axis_index("head")
    chip, core = lax.div(place, 2), lax.rem(place, 2)
    column = pl.multiple_of(2 * chip * width, width)
    loads = [
        copy(own.at[pl.ds(0, most), :], e0, sems.at[0]),
        copy(w.at[:, pl.ds(column, 2 * width)], weight, sems.at[1]),
    ]
    for shift, pack in ((1, e1), (2, e2), (3, e3), (0, e0)):
        group = lax.rem(chip + 4 - shift, 4)
        if shift == 0:
            for moved in loads:
                moved.wait()
        for head in range(2):
            slot = 2 * shift + head
            first = marks[shift, 0, head]
            for turn in range(3):
                block = pl.multiple_of(lax.rem(first + turn + 1, 4) * part, part)
                whole[pl.ds(block, part), half(slot)] = pack[turn * part : (turn + 1) * part, half(head)]
            whole[pl.ds(pl.multiple_of(first * part, part), part), half(slot)] = late[group, :part, half(head)]
            at = part
            for level in (1, 2):
                step = STEPS[level] // 4
                count = part // step
                mark = marks[shift, level, head]
                block = pl.multiple_of(lax.rem(mark, 4) * part, part)
                held = 2 * slot + level - 1
                wide[held] = whole[pl.ds(block, part), half(slot)].astype(F32)
                wide[held, pl.ds(lax.div(mark, 4), count, stride=step), :] = late[
                    group, at : at + count, half(head)
                ].astype(F32)
                whole[pl.ds(block, part), half(slot)] = wide[held].astype(BF16)
                at += count

    def product(which):
        total = 0.0
        for shift, pack in enumerate((None, e1, e2, e3)):
            if shift:
                chosen = pack[pl.ds(pl.multiple_of(most + 16 + which * width, 16), width), :]
            else:
                chosen = weight[:, pl.ds(pl.multiple_of(which * width, width), width)]
            total = total + jnp.dot(
                whole[:, shift * width : (shift + 1) * width], chosen, preferred_element_type=F32
            )
        return total

    send[...] = product(1 - core).astype(BF16)
    keep[...] = product(core)


def finish_kernel(keep, other, out, wide):
    part = keep.shape[0] // 4
    for head in range(2):
        for turn in range(4):
            block = slice(turn * part, (turn + 1) * part)
            wide[head, pl.ds(turn, part, stride=4), :] = keep[block, half(head)] + other[block, half(head)].astype(F32)
        out[:, half(head)] = wide[head].astype(BF16)


def shards(queries, keys, values, offsets, w_out):
    rows, width = queries.shape
    spread, heads = lax.axis_size("seq"), lax.axis_size("head")
    lines = spread // 4
    along_y = [[4 * line + y for y in range(4)] for line in range(lines)]
    far_lines = [[(4 * b + line) * 4 + y for b in range(4)] for line in range(4) for y in range(4)]
    along_x = [[2 * chip + core for chip in range(4)] for core in range(2)]
    dma = pltpu.SemaphoreType.DMA

    def swap(value, axis, groups):
        return lax.all_to_all(value, axis, 0, 0, axis_index_groups=groups)

    def shift_z(value, by):
        hops = [(4 * (4 * b + z) + y, 4 * (4 * b + (z + by) % 4) + y) for b in range(lines // 4) for z in range(4) for y in range(4)]
        return lax.ppermute(value, "seq", hops)

    def shift_x(value, by):
        return lax.ppermute(value, "head", [(place, (place + 2 * by) % heads) for place in range(heads)])

    count = [rows // step for step in STEPS]
    late_rows = sum(count)
    near_rows = 2 * count[0] + count[1] + count[2]
    z_rows = 2 * count[1] + 2 * count[2]
    queries, keys, values, offsets, w_out = map(stay, (queries, keys, values, offsets, w_out))
    near, near_z, own_q = call(
        pick_kernel,
        (pltpu.HBM((4, near_rows, width), BF16), pltpu.HBM((z_rows, width), BF16), pltpu.HBM((count[0], width), BF16)),
        [HBM] * 4,
        (HBM,) * 3,
        [
            pltpu.SMEM((2, 3), jnp.int32),
            pltpu.VMEM((3, rows, width), BF16),
            pltpu.VMEM((3, 2, rows, HEAD_DIM), F32),
            pltpu.VMEM((near_rows, width), BF16),
            pltpu.VMEM((z_rows, width), BF16),
            pltpu.VMEM((count[0], width), BF16),
            dma((13,)),
        ],
    )(offsets, queries, keys, values)
    zs = [stay(part) for part in [near_z] + [shift_z(near_z, by) for by in (1, 2, 3)]]
    near = swap(near, "seq", along_y)
    most = 3 * rows // 4
    packed = pltpu.HBM((most + 16 + 2 * width, width), BF16)
    kept = pltpu.HBM((2, late_rows, HEAD_DIM), F32)
    early, *packs, mixed, logs = call(
        local_kernel,
        (pltpu.HBM((most + 16, width), BF16), packed, packed, packed, kept, kept),
        [HBM] * 5,
        (HBM,) * 6,
        [
            pltpu.SMEM((2, 3), jnp.int32),
            pltpu.VMEM((3, rows, width), BF16),
            pltpu.VMEM((2, rows, HEAD_DIM), F32),
            pltpu.VMEM((most + 16, width), BF16),
            pltpu.VMEM((2, late_rows, HEAD_DIM), F32),
            pltpu.VMEM((2, late_rows, HEAD_DIM), F32),
            pltpu.VMEM(w_out.shape, BF16),
            dma((17,)),
        ],
    )(offsets, queries, keys, values, w_out)
    far_z = call(
        relay_kernel, pltpu.HBM((4, 4, 2 * count[2], width), BF16), [ANY] * 4 + [HBM, ANY], HBM, [pltpu.VMEM((4, 2 * count[2], width), BF16), dma((8,))]
    )(*zs, stay(early), near)
    far_z = swap(far_z, "seq", far_lines)
    packs = [shift_x(pack, by) for by, pack in enumerate(packs, 1)]
    marks = jnp.stack([part[most : most + 3, ::HEAD_DIM] for part in [early] + packs]).astype(jnp.int32)
    near_mixed, near_logs = call(
        near_kernel,
        (pltpu.HBM((2, count[0], HEAD_DIM), F32),) * 2,
        [HBM, ANY],
        (HBM,) * 2,
        [
            pltpu.VMEM((count[0], width), BF16),
            pltpu.VMEM((4, 2 * count[0], width), BF16),
            pltpu.VMEM((2, count[0], HEAD_DIM), F32),
            pltpu.VMEM((2, count[0], HEAD_DIM), F32),
            dma((4,)),
        ],
    )(stay(own_q), near)
    back = call(
        far_kernel,
        pltpu.HBM((4, count[1] + count[2], 3 * HEAD_DIM), F32),
        [ANY] * 6,
        HBM,
        [
            pltpu.VMEM((4, count[1] + count[2], width), BF16),
            pltpu.VMEM((4, 2 * count[1], width), BF16),
            pltpu.VMEM((4, 4, 2 * count[2], width), BF16),
            pltpu.VMEM((4, count[1] + count[2], 3 * HEAD_DIM), F32),
            dma((7,)),
        ],
    )(near, *zs, far_z)
    back = swap(back, "seq", along_y)
    late = call(
        merge_kernel,
        pltpu.HBM((4, late_rows, width), BF16),
        [HBM] * 5 + [ANY] * 4,
        HBM,
        [
            pltpu.SMEM((2, 3), jnp.int32),
            pltpu.VMEM(mixed.shape, F32),
            pltpu.VMEM(mixed.shape, F32),
            pltpu.VMEM(near_mixed.shape, F32),
            pltpu.VMEM(near_mixed.shape, F32),
            pltpu.VMEM(back.shape, F32),
            pltpu.VMEM((2, rows, HEAD_DIM), F32),
            pltpu.VMEM((2, rows, HEAD_DIM), F32),
            pltpu.VMEM((late_rows, width), BF16),
            dma((10,)),
        ],
    )(offsets, *map(stay, (mixed, logs, near_mixed, near_logs)), back, *packs)
    late = swap(late, "head", along_x)
    send, keep = call(
        project_kernel,
        (shape((rows, width), BF16), shape((rows, width), F32)),
        [SMEM, HBM] + [VMEM] * 4 + [HBM],
        (VMEM,) * 2,
        [
            pltpu.VMEM((most, width), BF16),
            pltpu.VMEM((16, count[0], HEAD_DIM), F32),
            pltpu.VMEM((rows, 4 * width), BF16),
            pltpu.VMEM((width, 2 * width), BF16),
            dma((2,)),
        ],
    )(marks, stay(early), *packs, late, w_out)
    other = lax.ppermute(send, "head", [(place, place ^ 1) for place in range(heads)])
    return call(
        finish_kernel,
        shape((rows, width), BF16),
        [VMEM] * 2,
        VMEM,
        [pltpu.VMEM((2, rows, HEAD_DIM), F32)],
    )(keep, other)


def solution(mesh):
    in_specs = (
        P("seq", "head"),
        P("seq", "head"),
        P("seq", "head"),
        P("head", None),
        P("head", None),
    )
    out_specs = P("seq", "head")
    return jax.shard_map(shards, mesh=mesh, in_specs=in_specs, out_specs=out_specs, check_vma=False)
```

```python
import math

import jax
import jax.numpy as jnp
from jax import lax
from jax.experimental import pallas as pl
from jax.experimental.pallas import tpu as pltpu
from jax.sharding import PartitionSpec as P

HEAD_DIM = 128
SCALE = HEAD_DIM ** (-0.5)
SCALE2 = SCALE * math.log2(math.e)
NEG = -1e30
F32 = jnp.float32
BF16 = jnp.bfloat16
STEPS = (4, 16, 64)
VMEM = pl.BlockSpec(memory_space=pltpu.VMEM)
SMEM = pl.BlockSpec(memory_space=pltpu.SMEM)
HBM = pl.BlockSpec(memory_space=pltpu.HBM)
ANY = pl.BlockSpec(memory_space=pl.ANY)
PARAMS = pltpu.CompilerParams(vmem_limit_bytes=20 << 20)


def half(head):
    return slice(head * HEAD_DIM, (head + 1) * HEAD_DIM)


def rows_of(offset, total, step):
    return pl.ds(offset, total // step, stride=step)


def call(kernel, out, in_specs, out_specs, scratch=()):
    return pl.pallas_call(
        kernel,
        out_shape=out,
        in_specs=in_specs,
        out_specs=out_specs,
        scratch_shapes=scratch,
        compiler_params=PARAMS,
    )


def shape(dims, dtype):
    return jax.ShapeDtypeStruct(dims, dtype)


def stay(value):
    return pltpu.with_memory_space_constraint(value, pltpu.HBM)


def copy(source, target, sem):
    moved = pltpu.make_async_copy(source, target, sem)
    moved.start()
    return moved


def attend(queries, keys, values, kept):
    scores = lax.dot_general(queries, keys, (((1,), (1,)), ((), ())), preferred_element_type=F32)
    scores = jnp.where(kept, scores, NEG)
    top = jnp.max(scores, axis=-1, keepdims=True)
    weights = jnp.where(kept, jnp.exp2((scores - top) * SCALE2), 0.0)
    total = jnp.sum(weights, axis=-1, keepdims=True)
    some = total > 0.0
    safe = jnp.where(some, total, 1.0)
    out = jnp.dot(weights.astype(BF16), values, preferred_element_type=F32) / safe
    return out, jnp.where(some, top * SCALE + jnp.log(safe), NEG)


def pick_kernel(off_in, q, k, v, near_out, near_z, own_q, off, raw, wide, near, pack, query, sems):
    rows = q.shape[0]
    count = [rows // step for step in STEPS]
    first = copy(off_in, off, sems.at[0])
    loads = [copy(source, raw.at[slot], sems.at[1 + slot]) for slot, source in enumerate((k, v, q))]
    moves = []
    first.wait()
    for slot in range(3):
        loads[slot].wait()
        for head in range(2):
            wide[slot, head] = raw[slot, :, half(head)].astype(F32)
            picks = [
                wide[slot, head, rows_of(off[head, level], rows, step), :].astype(BF16)
                for level, step in enumerate(STEPS)
            ]
            if slot < 2:
                near[slot * count[0] : (slot + 1) * count[0], half(head)] = picks[0]
                pack[slot * count[1] : (slot + 1) * count[1], half(head)] = picks[1]
                at = 2 * count[1] + slot * count[2]
                pack[at : at + count[2], half(head)] = picks[2]
            else:
                query[:, half(head)] = picks[0]
                at = 2 * count[0]
                near[at : at + count[1], half(head)] = picks[1]
                near[at + count[1] : at + count[1] + count[2], half(head)] = picks[2]
        if slot == 1:
            moves = [copy(pack, near_z, sems.at[4])]
    moves.append(copy(query, own_q, sems.at[8]))
    moves += [copy(near, near_out.at[target], sems.at[9 + target]) for target in range(4)]
    for moved in moves:
        moved.wait()


def relay_kernel(z0, z1, z2, z3, _1, _2, far_z, part, sems):
    line = lax.rem(lax.div(lax.axis_index("seq"), 4), 4)
    loads = [
        copy(z.at[pl.ds(128, 32), :], part.at[lax.rem(line + 4 - shift, 4)], sems.at[shift])
        for shift, z in enumerate((z0, z1, z2, z3))
    ]
    for moved in loads:
        moved.wait()
    moves = [copy(part, far_z.at[target], sems.at[4 + target]) for target in range(far_z.shape[0])]
    for moved in moves:
        moved.wait()


def local_kernel(off_in, q, k, v, w, own, out1, out2, out3, mixed, logs, off, raw, wide, early, some, some_logs, held, sems):
    chip = lax.div(lax.axis_index("head"), 2)
    rows, width = q.shape
    block = 512
    part = rows // 4
    first_copy = copy(off_in, off, sems.at[0])
    loads = []
    for head in range(2):
        for slot, source in enumerate((q, k, v)):
            loads.append(copy(source.at[:, pl.ds(head * HEAD_DIM, HEAD_DIM)], raw.at[head, slot], sems.at[1 + 3 * head + slot]))
    column = copy(w, held, sems.at[7])
    row = lax.broadcasted_iota(jnp.int32, (block, block), 0)
    kept = lax.broadcasted_iota(jnp.int32, (block, block), 1) <= row
    line = lax.broadcasted_iota(jnp.int32, (16, HEAD_DIM), 0)
    moves = []
    first_copy.wait()
    for head in range(2):
        for moved in loads[3 * head : 3 * head + 3]:
            moved.wait()
        for first in range(0, rows, block):
            last = first + block
            query = raw[head, 0, first:last, :]
            pieces = [(first, last)] + ([(0, first)] if first else [])
            scores = [
                lax.dot_general(query, raw[head, 1, low:high, :], (((1,), (1,)), ((), ())), preferred_element_type=F32)
                for low, high in pieces
            ]
            scores[0] = jnp.where(kept, scores[0], NEG)
            top = jnp.max(scores[0], axis=-1, keepdims=True)
            for piece in scores[1:]:
                top = jnp.maximum(top, jnp.max(piece, axis=-1, keepdims=True))
            total, out = 0.0, 0.0
            for piece, (low, high) in zip(scores, pieces):
                weights = jnp.exp2((piece - top) * SCALE2)
                total = total + jnp.sum(weights, axis=-1, keepdims=True)
                out = out + jnp.dot(weights.astype(BF16), raw[head, 2, low:high, :], preferred_element_type=F32)
            wide[head, 0, first:last, :] = out / total
            wide[head, 1, first:last, :] = jnp.broadcast_to(top * SCALE + jnp.log(total), out.shape)
        for turn in range(3):
            where = rows_of(lax.rem(off[head, 0] + turn + 1, 4), rows, 4)
            early[turn * part : (turn + 1) * part, half(head)] = wide[head, 0, where, :].astype(BF16)
        marks = jnp.where(line == 0, off[head, 0], jnp.where(line == 1, off[head, 1], off[head, 2]))
        early[3 * part :, half(head)] = marks.astype(F32).astype(BF16)
        at = 0
        for level, step in enumerate(STEPS):
            count = rows // step
            where = rows_of(off[head, level], rows, step)
            some[head, at : at + count, :] = wide[head, 0, where, :]
            some_logs[head, at : at + count, :] = wide[head, 1, where, :]
            at += count
        lanes = pl.ds(head * HEAD_DIM, HEAD_DIM)
        for slot, target in enumerate((own, out1, out2, out3)):
            place = target.at[pl.ds(0, 3 * part + 16), lanes]
            moves.append(copy(early.at[:, lanes], place, sems.at[8 + 4 * head + slot]))
        moves.append(copy(some.at[head], mixed.at[head], sems.at[16 + 2 * head]))
        moves.append(copy(some_logs.at[head], logs.at[head], sems.at[17 + 2 * head]))
        if head == 0:
            column.wait()
            for shift, target in enumerate((out1, out2, out3), 1):
                for side in range(2):
                    place = pl.multiple_of((2 * lax.rem(chip + shift, 4) + side) * width, width)
                    at = 3 * part + 16 + side * width
                    sem = sems.at[18 + 2 * shift + side]
                    moves.append(copy(held.at[:, pl.ds(place, width)], target.at[pl.ds(at, width), :], sem))
    for moved in moves:
        moved.wait()


def merge(parts):
    top = parts[0][1]
    for _, log in parts[1:]:
        top = jnp.maximum(top, log)
    total, out = 0.0, 0.0
    for value, log in parts:
        share = jnp.exp(log - top)
        total = total + share
        out = out + share * value
    return out / total, top + jnp.log(total)


def spread_rows(off, head, packed, wide):
    rows, at = wide.shape[1], 0
    for level, step in enumerate(STEPS):
        count = rows // step
        wide[head, rows_of(off[head, level], rows, step), :] = packed[head, at : at + count, :]
        at += count


def gather_rows(off, head, wide, packed):
    rows, at = wide.shape[1], 0
    for level, step in enumerate(STEPS):
        count = rows // step
        packed[head, at : at + count, :] = wide[head, rows_of(off[head, level], rows, step), :].astype(packed.dtype)
        at += count


def near_kernel(
    off_in, own_q, near_in, m_in, l_in, m_out, l_out, off, queries, near, mixed, logs, run, run_logs, sems
):
    count = own_q.shape[0]
    rows = 4 * count
    places = ((off_in, off), (own_q, queries), (near_in.at[:, pl.ds(0, 2 * count), :], near), (m_in, mixed), (l_in, logs))
    loads = [copy(source, target, sems.at[slot]) for slot, (source, target) in enumerate(places)]
    for moved in loads:
        moved.wait()
    mine = lax.rem(lax.axis_index("seq"), 4)
    for head in range(2):
        keys = near[:, :count, half(head)].reshape(-1, HEAD_DIM)
        values = near[:, count:, half(head)].reshape(-1, HEAD_DIM)
        dims = (count, 4 * count)
        query = mine * count + lax.broadcasted_iota(jnp.int32, dims, 0)
        key = lax.broadcasted_iota(jnp.int32, dims, 1)
        out, log = attend(queries[:, half(head)], keys, values, key <= query)
        log = jnp.broadcast_to(log, out.shape)
        out, log = merge([(mixed[head, :count, :], logs[head, :count, :]), (out, log)])
        spread_rows(off, head, mixed, run)
        spread_rows(off, head, logs, run_logs)
        where = rows_of(off[head, 0], rows, 4)
        run[head, where, :] = out
        run_logs[head, where, :] = log
        gather_rows(off, head, run, mixed)
        gather_rows(off, head, run_logs, logs)
    moves = [copy(mixed, m_out, sems.at[0]), copy(logs, l_out, sems.at[1])]
    for moved in moves:
        moved.wait()


def far_kernel(near_in, z0, z1, z2, z3, hi, _, back, near, zs, part, sems):
    seq = lax.axis_index("seq")
    mine, line = lax.rem(seq, 4), lax.div(seq, 4)
    loads = [copy(z.at[pl.ds(0, 128), :], zs.at[shift], sems.at[2 + shift]) for shift, z in enumerate((z0, z1, z2, z3))]
    loads.append(copy(near_in.at[:, pl.ds(512, 80), :], near, sems.at[0]))
    for moved in loads:
        moved.wait()
    at = 0
    for level, count in ((1, 64), (2, 16)):
        place = lax.rem(line, 4) if level == 1 else line
        logs = []
        for head in range(2):
            queries = near[:, at : at + count, half(head)].reshape(-1, HEAD_DIM)
            if level == 1:
                keys = zs[:, :count, half(head)].reshape(-1, HEAD_DIM)
                values = zs[:, count:, half(head)].reshape(-1, HEAD_DIM)
            else:
                keys = hi[:, :, :count, half(head)].reshape(-1, HEAD_DIM)
                values = hi[:, :, count:, half(head)].reshape(-1, HEAD_DIM)
            dims = (4 * count, keys.shape[0])
            row = lax.broadcasted_iota(jnp.int32, dims, 0)
            query = place * 4 * count + row
            key = lax.broadcasted_iota(jnp.int32, dims, 1)
            source = lax.rem(place + 4 - lax.div(key, count), 4) if level == 1 else lax.div(key, count)
            key = (source * 4 + mine) * count + lax.rem(key, count)
            out, log = attend(queries, keys, values, key <= query)
            logs.append(log)
            part[:, at : at + count, half(head)] = out.reshape(4, count, HEAD_DIM).astype(BF16)
        lane = lax.broadcasted_iota(jnp.int32, (4 * count, HEAD_DIM), 1)
        left = jnp.where(lane < HEAD_DIM // 2, logs[0], logs[1])
        both = left.astype(BF16)
        for piece in range(1, 3):
            left = left - left.astype(BF16).astype(F32)
            both = jnp.where(lax.rem(lane, HEAD_DIM // 2) < 16 * piece, both, left.astype(BF16))
        part[:, at : at + count, 2 * HEAD_DIM :] = both.reshape(4, count, HEAD_DIM)
        at += count
    moves = [copy(part, back, sems.at[1])]
    for moved in moves:
        moved.wait()


def merge_kernel(off_in, m_in, l_in, back, _1, _2, late, off, mixed, logs, run, run_logs, pack, sems):
    rows = run.shape[1]
    places = ((off_in, off), (m_in, mixed), (l_in, logs))
    loads = [copy(source, target, sems.at[slot]) for slot, (source, target) in enumerate(places)]
    for moved in loads:
        moved.wait()
    for head in range(2):
        spread_rows(off, head, mixed, run)
        spread_rows(off, head, logs, run_logs)
        at = 0
        for level in (1, 2):
            count = rows // STEPS[level]
            where = rows_of(off[head, level], rows, STEPS[level])
            parts = [(run[head, where, :], run_logs[head, where, :])]
            for source in range(4):
                lane = head * (HEAD_DIM // 2)
                pieces = back[source, at : at + count, 2 * HEAD_DIM :].astype(F32)
                log = sum(pieces[:, lane + 16 * piece : lane + 16 * piece + 1] for piece in range(3))
                value = back[source, at : at + count, half(head)].astype(F32)
                parts.append((value, jnp.broadcast_to(log, (count, HEAD_DIM))))
            at += count
            out, log = merge(parts)
            run[head, where, :] = out
            run_logs[head, where, :] = log
        at = 0
        for level, step in enumerate(STEPS):
            count = rows // step
            pack[at : at + count, half(head)] = run[head, rows_of(off[head, level], rows, step), :].astype(BF16)
            at += count
    moves = [copy(pack, late.at[target], sems.at[target]) for target in range(4)]
    for moved in moves:
        moved.wait()


def project_kernel(marks, own, e1, e2, e3, late, w, send, keep, e0, wide, whole, weight, sems):
    rows, width = keep.shape
    part = rows // 4
    most = 3 * part
    place = lax.axis_index("head")
    chip, core = lax.div(place, 2), lax.rem(place, 2)
    column = pl.multiple_of(2 * chip * width, width)
    loads = [
        copy(own.at[pl.ds(0, most), :], e0, sems.at[0]),
        copy(w.at[:, pl.ds(column, 2 * width)], weight, sems.at[1]),
    ]
    for shift, pack in ((1, e1), (2, e2), (3, e3), (0, e0)):
        group = lax.rem(chip + 4 - shift, 4)
        if shift == 0:
            for moved in loads:
                moved.wait()
        for head in range(2):
            slot = 2 * shift + head
            first = marks[shift, 0, head]
            for turn in range(3):
                block = pl.multiple_of(lax.rem(first + turn + 1, 4) * part, part)
                whole[pl.ds(block, part), half(slot)] = pack[turn * part : (turn + 1) * part, half(head)]
            whole[pl.ds(pl.multiple_of(first * part, part), part), half(slot)] = late[group, :part, half(head)]
            at = part
            for level in (1, 2):
                step = STEPS[level] // 4
                count = part // step
                mark = marks[shift, level, head]
                block = pl.multiple_of(lax.rem(mark, 4) * part, part)
                held = 2 * slot + level - 1
                wide[held] = whole[pl.ds(block, part), half(slot)].astype(F32)
                wide[held, pl.ds(lax.div(mark, 4), count, stride=step), :] = late[
                    group, at : at + count, half(head)
                ].astype(F32)
                whole[pl.ds(block, part), half(slot)] = wide[held].astype(BF16)
                at += count

    def product(which):
        total = 0.0
        for shift, pack in enumerate((None, e1, e2, e3)):
            if shift:
                chosen = pack[pl.ds(pl.multiple_of(most + 16 + which * width, 16), width), :]
            else:
                chosen = weight[:, pl.ds(pl.multiple_of(which * width, width), width)]
            total = total + jnp.dot(
                whole[:, shift * width : (shift + 1) * width], chosen, preferred_element_type=F32
            )
        return total

    send[...] = product(1 - core).astype(BF16)
    keep[...] = product(core)


def finish_kernel(keep, other, out, wide):
    part = keep.shape[0] // 4
    for head in range(2):
        for turn in range(4):
            block = slice(turn * part, (turn + 1) * part)
            wide[head, pl.ds(turn, part, stride=4), :] = keep[block, half(head)] + other[block, half(head)].astype(F32)
        out[:, half(head)] = wide[head].astype(BF16)


def shards(queries, keys, values, offsets, w_out):
    rows, width = queries.shape
    spread, heads = lax.axis_size("seq"), lax.axis_size("head")
    lines = spread // 4
    along_y = [[4 * line + y for y in range(4)] for line in range(lines)]
    far_lines = [[(4 * b + line) * 4 + y for b in range(4)] for line in range(4) for y in range(4)]
    along_x = [[2 * chip + core for chip in range(4)] for core in range(2)]
    dma = pltpu.SemaphoreType.DMA

    def swap(value, axis, groups):
        return lax.all_to_all(value, axis, 0, 0, axis_index_groups=groups)

    def shift_z(value, by):
        hops = [(4 * (4 * b + z) + y, 4 * (4 * b + (z + by) % 4) + y) for b in range(lines // 4) for z in range(4) for y in range(4)]
        return lax.ppermute(value, "seq", hops)

    def shift_x(value, by):
        return lax.ppermute(value, "head", [(place, (place + 2 * by) % heads) for place in range(heads)])

    count = [rows // step for step in STEPS]
    late_rows = sum(count)
    near_rows = 2 * count[0] + count[1] + count[2]
    z_rows = 2 * count[1] + 2 * count[2]
    queries, keys, values, offsets, w_out = map(stay, (queries, keys, values, offsets, w_out))
    near, near_z, own_q = call(
        pick_kernel,
        (pltpu.HBM((4, near_rows, width), BF16), pltpu.HBM((z_rows, width), BF16), pltpu.HBM((count[0], width), BF16)),
        [HBM] * 4,
        (HBM,) * 3,
        [
            pltpu.SMEM((2, 3), jnp.int32),
            pltpu.VMEM((3, rows, width), BF16),
            pltpu.VMEM((3, 2, rows, HEAD_DIM), F32),
            pltpu.VMEM((near_rows, width), BF16),
            pltpu.VMEM((z_rows, width), BF16),
            pltpu.VMEM((count[0], width), BF16),
            dma((13,)),
        ],
    )(offsets, queries, keys, values)
    zs = [stay(part) for part in [near_z] + [shift_z(near_z, by) for by in (1, 2, 3)]]
    near = swap(near, "seq", along_y)
    most = 3 * rows // 4
    packed = pltpu.HBM((most + 16 + 2 * width, width), BF16)
    kept = pltpu.HBM((2, late_rows, HEAD_DIM), F32)
    early, *packs, mixed, logs = call(
        local_kernel,
        (pltpu.HBM((most + 16, width), BF16), packed, packed, packed, kept, kept),
        [HBM] * 5,
        (HBM,) * 6,
        [
            pltpu.SMEM((2, 3), jnp.int32),
            pltpu.VMEM((2, 3, rows, HEAD_DIM), BF16),
            pltpu.VMEM((2, 2, rows, HEAD_DIM), F32),
            pltpu.VMEM((most + 16, width), BF16),
            pltpu.VMEM((2, late_rows, HEAD_DIM), F32),
            pltpu.VMEM((2, late_rows, HEAD_DIM), F32),
            pltpu.VMEM(w_out.shape, BF16),
            dma((26,)),
        ],
    )(offsets, queries, keys, values, w_out)
    far_z = call(
        relay_kernel, pltpu.HBM((4, 4, 2 * count[2], width), BF16), [ANY] * 4 + [HBM, ANY], HBM, [pltpu.VMEM((4, 2 * count[2], width), BF16), dma((8,))]
    )(*zs, stay(early), near)
    far_z = swap(far_z, "seq", far_lines)
    packs = [shift_x(pack, by) for by, pack in enumerate(packs, 1)]
    marks = jnp.stack([part[most : most + 3, ::HEAD_DIM] for part in [early] + packs]).astype(jnp.int32)
    mixed, logs = call(
        near_kernel,
        (kept, kept),
        [HBM] * 2 + [ANY] + [HBM] * 2,
        (HBM,) * 2,
        [
            pltpu.SMEM((2, 3), jnp.int32),
            pltpu.VMEM((count[0], width), BF16),
            pltpu.VMEM((4, 2 * count[0], width), BF16),
            pltpu.VMEM(mixed.shape, F32),
            pltpu.VMEM(mixed.shape, F32),
            pltpu.VMEM((2, rows, HEAD_DIM), F32),
            pltpu.VMEM((2, rows, HEAD_DIM), F32),
            dma((5,)),
        ],
    )(offsets, stay(own_q), near, stay(mixed), stay(logs))
    back = call(
        far_kernel,
        pltpu.HBM((4, count[1] + count[2], 3 * HEAD_DIM), BF16),
        [ANY] * 5 + [VMEM, HBM],
        HBM,
        [
            pltpu.VMEM((4, count[1] + count[2], width), BF16),
            pltpu.VMEM((4, 2 * count[1], width), BF16),
            pltpu.VMEM((4, count[1] + count[2], 3 * HEAD_DIM), BF16),
            dma((7,)),
        ],
    )(near, *zs, far_z, stay(mixed))
    back = swap(back, "seq", along_y)
    late = call(
        merge_kernel,
        pltpu.HBM((4, late_rows, width), BF16),
        [HBM] * 3 + [VMEM] + [ANY] * 2,
        HBM,
        [
            pltpu.SMEM((2, 3), jnp.int32),
            pltpu.VMEM(mixed.shape, F32),
            pltpu.VMEM(mixed.shape, F32),
            pltpu.VMEM((2, rows, HEAD_DIM), F32),
            pltpu.VMEM((2, rows, HEAD_DIM), F32),
            pltpu.VMEM((late_rows, width), BF16),
            dma((4,)),
        ],
    )(offsets, stay(mixed), stay(logs), back, packs[0], packs[2])
    late = swap(late, "head", along_x)
    send, keep = call(
        project_kernel,
        (shape((rows, width), BF16), shape((rows, width), F32)),
        [SMEM, HBM] + [VMEM] * 4 + [HBM],
        (VMEM,) * 2,
        [
            pltpu.VMEM((most, width), BF16),
            pltpu.VMEM((16, count[0], HEAD_DIM), F32),
            pltpu.VMEM((rows, 4 * width), BF16),
            pltpu.VMEM((width, 2 * width), BF16),
            dma((2,)),
        ],
    )(marks, stay(early), *packs, late, w_out)
    other = lax.ppermute(send, "head", [(place, place ^ 1) for place in range(heads)])
    return call(
        finish_kernel,
        shape((rows, width), BF16),
        [VMEM] * 2,
        VMEM,
        [pltpu.VMEM((2, rows, HEAD_DIM), F32)],
    )(keep, other)


def solution(mesh):
    in_specs = (
        P("seq", "head"),
        P("seq", "head"),
        P("seq", "head"),
        P("head", None),
        P("head", None),
    )
    out_specs = P("seq", "head")
    return jax.shard_map(shards, mesh=mesh, in_specs=in_specs, out_specs=out_specs, check_vma=False)
```

```python
import math

import jax
import jax.numpy as jnp
from jax import lax
from jax.experimental import pallas as pl
from jax.experimental.pallas import tpu as pltpu
from jax.sharding import PartitionSpec as P

HEAD_DIM = 128
SCALE = HEAD_DIM ** (-0.5)
SCALE2 = SCALE * math.log2(math.e)
NEG = -1e30
F32 = jnp.float32
BF16 = jnp.bfloat16
STEPS = (4, 16, 64)
VMEM = pl.BlockSpec(memory_space=pltpu.VMEM)
SMEM = pl.BlockSpec(memory_space=pltpu.SMEM)
HBM = pl.BlockSpec(memory_space=pltpu.HBM)
ANY = pl.BlockSpec(memory_space=pl.ANY)
PARAMS = pltpu.CompilerParams(vmem_limit_bytes=20 << 20)


def half(head):
    return slice(head * HEAD_DIM, (head + 1) * HEAD_DIM)


def rows_of(offset, total, step):
    return pl.ds(offset, total // step, stride=step)


def call(kernel, out, in_specs, out_specs, scratch=()):
    return pl.pallas_call(
        kernel,
        out_shape=out,
        in_specs=in_specs,
        out_specs=out_specs,
        scratch_shapes=scratch,
        compiler_params=PARAMS,
    )


def shape(dims, dtype):
    return jax.ShapeDtypeStruct(dims, dtype)


def stay(value):
    return pltpu.with_memory_space_constraint(value, pltpu.HBM)


def copy(source, target, sem):
    moved = pltpu.make_async_copy(source, target, sem)
    moved.start()
    return moved


def attend(queries, keys, values, kept):
    scores = lax.dot_general(queries, keys, (((1,), (1,)), ((), ())), preferred_element_type=F32)
    scores = jnp.where(kept, scores, NEG)
    top = jnp.max(scores, axis=-1, keepdims=True)
    weights = jnp.where(kept, jnp.exp2((scores - top) * SCALE2), 0.0)
    total = jnp.sum(weights, axis=-1, keepdims=True)
    some = total > 0.0
    safe = jnp.where(some, total, 1.0)
    out = jnp.dot(weights.astype(BF16), values, preferred_element_type=F32) / safe
    return out, jnp.where(some, top * SCALE + jnp.log(safe), NEG)


def pick_kernel(off_in, q, k, v, near_out, near_z, own_q, off, raw, wide, near, pack, query, sems):
    rows = q.shape[0]
    count = [rows // step for step in STEPS]
    first = copy(off_in, off, sems.at[0])
    loads = [copy(source, raw.at[slot], sems.at[1 + slot]) for slot, source in enumerate((k, v, q))]
    moves = []
    first.wait()
    for slot in range(3):
        loads[slot].wait()
        for head in range(2):
            wide[slot, head] = raw[slot, :, half(head)].astype(F32)
            picks = [
                wide[slot, head, rows_of(off[head, level], rows, step), :].astype(BF16)
                for level, step in enumerate(STEPS)
            ]
            if slot < 2:
                near[slot * count[0] : (slot + 1) * count[0], half(head)] = picks[0]
                pack[slot * count[1] : (slot + 1) * count[1], half(head)] = picks[1]
                at = 2 * count[1] + slot * count[2]
                pack[at : at + count[2], half(head)] = picks[2]
            else:
                query[:, half(head)] = picks[0]
                at = 2 * count[0]
                near[at : at + count[1], half(head)] = picks[1]
                near[at + count[1] : at + count[1] + count[2], half(head)] = picks[2]
        if slot == 1:
            moves = [copy(pack, near_z, sems.at[4])]
    moves.append(copy(query, own_q, sems.at[8]))
    moves += [copy(near, near_out.at[target], sems.at[9 + target]) for target in range(4)]
    for moved in moves:
        moved.wait()


def relay_kernel(z0, z1, z2, z3, _1, _2, far_z, part, sems):
    line = lax.rem(lax.div(lax.axis_index("seq"), 4), 4)
    loads = [
        copy(z.at[pl.ds(128, 32), :], part.at[lax.rem(line + 4 - shift, 4)], sems.at[shift])
        for shift, z in enumerate((z0, z1, z2, z3))
    ]
    for moved in loads:
        moved.wait()
    moves = [copy(part, far_z.at[target], sems.at[4 + target]) for target in range(far_z.shape[0])]
    for moved in moves:
        moved.wait()


def local_kernel(off_in, q, k, v, w, own, out1, out2, out3, mixed, logs, off, raw, wide, early, some, some_logs, held, sems):
    chip = lax.div(lax.axis_index("head"), 2)
    rows, width = q.shape
    block = 512
    part = rows // 4
    first_copy = copy(off_in, off, sems.at[0])
    loads = []
    for head in range(2):
        for slot, source in enumerate((q, k, v)):
            loads.append(copy(source.at[:, pl.ds(head * HEAD_DIM, HEAD_DIM)], raw.at[head, slot], sems.at[1 + 3 * head + slot]))
    column = copy(w, held, sems.at[7])
    row = lax.broadcasted_iota(jnp.int32, (block, block), 0)
    kept = lax.broadcasted_iota(jnp.int32, (block, block), 1) <= row
    line = lax.broadcasted_iota(jnp.int32, (16, HEAD_DIM), 0)
    moves = []
    first_copy.wait()
    for head in range(2):
        for moved in loads[3 * head : 3 * head + 3]:
            moved.wait()
        for first in range(0, rows, block):
            last = first + block
            query = raw[head, 0, first:last, :]
            pieces = [(first, last)] + ([(0, first)] if first else [])
            scores = [
                lax.dot_general(query, raw[head, 1, low:high, :], (((1,), (1,)), ((), ())), preferred_element_type=F32)
                for low, high in pieces
            ]
            scores[0] = jnp.where(kept, scores[0], NEG)
            top = jnp.max(scores[0], axis=-1, keepdims=True)
            for piece in scores[1:]:
                top = jnp.maximum(top, jnp.max(piece, axis=-1, keepdims=True))
            total, out = 0.0, 0.0
            for piece, (low, high) in zip(scores, pieces):
                weights = jnp.exp2((piece - top) * SCALE2)
                total = total + jnp.sum(weights, axis=-1, keepdims=True)
                out = out + jnp.dot(weights.astype(BF16), raw[head, 2, low:high, :], preferred_element_type=F32)
            wide[head, 0, first:last, :] = out / total
            wide[head, 1, first:last, :] = jnp.broadcast_to(top * SCALE + jnp.log(total), out.shape)
        for turn in range(3):
            where = rows_of(lax.rem(off[head, 0] + turn + 1, 4), rows, 4)
            early[turn * part : (turn + 1) * part, half(head)] = wide[head, 0, where, :].astype(BF16)
        marks = jnp.where(line == 0, off[head, 0], jnp.where(line == 1, off[head, 1], off[head, 2]))
        early[3 * part :, half(head)] = marks.astype(F32).astype(BF16)
        at = 0
        for level, step in enumerate(STEPS):
            count = rows // step
            where = rows_of(off[head, level], rows, step)
            some[head, at : at + count, :] = wide[head, 0, where, :]
            some_logs[head, at : at + count, :] = wide[head, 1, where, :]
            at += count
        lanes = pl.ds(head * HEAD_DIM, HEAD_DIM)
        for slot, target in enumerate((own, out1, out2, out3)):
            place = target.at[pl.ds(0, 3 * part + 16), lanes]
            moves.append(copy(early.at[:, lanes], place, sems.at[8 + 4 * head + slot]))
        moves.append(copy(some.at[head], mixed.at[head], sems.at[16 + 2 * head]))
        moves.append(copy(some_logs.at[head], logs.at[head], sems.at[17 + 2 * head]))
        if head == 0:
            column.wait()
            for shift, target in enumerate((out1, out2, out3), 1):
                for side in range(2):
                    place = pl.multiple_of((2 * lax.rem(chip + shift, 4) + side) * width, width)
                    at = 3 * part + 16 + side * width
                    sem = sems.at[18 + 2 * shift + side]
                    moves.append(copy(held.at[:, pl.ds(place, width)], target.at[pl.ds(at, width), :], sem))
    for moved in moves:
        moved.wait()


def merge(parts):
    top = parts[0][1]
    for _, log in parts[1:]:
        top = jnp.maximum(top, log)
    total, out = 0.0, 0.0
    for value, log in parts:
        share = jnp.exp(log - top)
        total = total + share
        out = out + share * value
    return out / total, top + jnp.log(total)


def spread_rows(off, head, packed, wide):
    rows, at = wide.shape[1], 0
    for level, step in enumerate(STEPS):
        count = rows // step
        wide[head, rows_of(off[head, level], rows, step), :] = packed[head, at : at + count, :]
        at += count


def gather_rows(off, head, wide, packed):
    rows, at = wide.shape[1], 0
    for level, step in enumerate(STEPS):
        count = rows // step
        packed[head, at : at + count, :] = wide[head, rows_of(off[head, level], rows, step), :].astype(packed.dtype)
        at += count


def near_kernel(
    off_in, own_q, near_in, m_in, l_in, m_out, l_out, off, queries, near, mixed, logs, run, run_logs, sems
):
    count = own_q.shape[0]
    rows = 4 * count
    places = ((off_in, off), (own_q, queries), (near_in.at[:, pl.ds(0, 2 * count), :], near), (m_in, mixed), (l_in, logs))
    loads = [copy(source, target, sems.at[slot]) for slot, (source, target) in enumerate(places)]
    for moved in loads:
        moved.wait()
    mine = lax.rem(lax.axis_index("seq"), 4)
    for head in range(2):
        keys = near[:, :count, half(head)].reshape(-1, HEAD_DIM)
        values = near[:, count:, half(head)].reshape(-1, HEAD_DIM)
        dims = (count, 4 * count)
        query = mine * count + lax.broadcasted_iota(jnp.int32, dims, 0)
        key = lax.broadcasted_iota(jnp.int32, dims, 1)
        out, log = attend(queries[:, half(head)], keys, values, key <= query)
        log = jnp.broadcast_to(log, out.shape)
        out, log = merge([(mixed[head, :count, :], logs[head, :count, :]), (out, log)])
        spread_rows(off, head, mixed, run)
        spread_rows(off, head, logs, run_logs)
        where = rows_of(off[head, 0], rows, 4)
        run[head, where, :] = out
        run_logs[head, where, :] = log
        gather_rows(off, head, run, mixed)
        gather_rows(off, head, run_logs, logs)
    moves = [copy(mixed, m_out, sems.at[0]), copy(logs, l_out, sems.at[1])]
    for moved in moves:
        moved.wait()


def far_kernel(near_in, z0, z1, z2, z3, hi, _, back, near, zs, part, sems):
    seq = lax.axis_index("seq")
    mine, line = lax.rem(seq, 4), lax.div(seq, 4)
    loads = [copy(z.at[pl.ds(0, 128), :], zs.at[shift], sems.at[2 + shift]) for shift, z in enumerate((z0, z1, z2, z3))]
    loads.append(copy(near_in.at[:, pl.ds(512, 80), :], near, sems.at[0]))
    for moved in loads:
        moved.wait()
    at = 0
    for level, count in ((1, 64), (2, 16)):
        place = lax.rem(line, 4) if level == 1 else line
        logs = []
        for head in range(2):
            queries = near[:, at : at + count, half(head)].reshape(-1, HEAD_DIM)
            if level == 1:
                keys = zs[:, :count, half(head)].reshape(-1, HEAD_DIM)
                values = zs[:, count:, half(head)].reshape(-1, HEAD_DIM)
            else:
                keys = hi[:, :, :count, half(head)].reshape(-1, HEAD_DIM)
                values = hi[:, :, count:, half(head)].reshape(-1, HEAD_DIM)
            dims = (4 * count, keys.shape[0])
            row = lax.broadcasted_iota(jnp.int32, dims, 0)
            query = place * 4 * count + row
            key = lax.broadcasted_iota(jnp.int32, dims, 1)
            source = lax.rem(place + 4 - lax.div(key, count), 4) if level == 1 else lax.div(key, count)
            key = (source * 4 + mine) * count + lax.rem(key, count)
            out, log = attend(queries, keys, values, key <= query)
            logs.append(log)
            part[:, at : at + count, half(head)] = out.reshape(4, count, HEAD_DIM).astype(BF16)
        lane = lax.broadcasted_iota(jnp.int32, (4 * count, HEAD_DIM), 1)
        left = jnp.where(lane < HEAD_DIM // 2, logs[0], logs[1])
        both = left.astype(BF16)
        for piece in range(1, 3):
            left = left - left.astype(BF16).astype(F32)
            both = jnp.where(lax.rem(lane, HEAD_DIM // 2) < 16 * piece, both, left.astype(BF16))
        part[:, at : at + count, 2 * HEAD_DIM :] = both.reshape(4, count, HEAD_DIM)
        at += count
    moves = [copy(part, back, sems.at[1])]
    for moved in moves:
        moved.wait()


def merge_kernel(off_in, m_in, l_in, back, late, off, mixed, logs, run, run_logs, pack, sems):
    rows = run.shape[1]
    places = ((off_in, off), (m_in, mixed), (l_in, logs))
    loads = [copy(source, target, sems.at[slot]) for slot, (source, target) in enumerate(places)]
    for moved in loads:
        moved.wait()
    for head in range(2):
        spread_rows(off, head, mixed, run)
        spread_rows(off, head, logs, run_logs)
        at = 0
        for level in (1, 2):
            count = rows // STEPS[level]
            where = rows_of(off[head, level], rows, STEPS[level])
            parts = [(run[head, where, :], run_logs[head, where, :])]
            for source in range(4):
                lane = head * (HEAD_DIM // 2)
                pieces = back[source, at : at + count, 2 * HEAD_DIM :].astype(F32)
                log = sum(pieces[:, lane + 16 * piece : lane + 16 * piece + 1] for piece in range(3))
                value = back[source, at : at + count, half(head)].astype(F32)
                parts.append((value, jnp.broadcast_to(log, (count, HEAD_DIM))))
            at += count
            out, log = merge(parts)
            run[head, where, :] = out
            run_logs[head, where, :] = log
        at = 0
        for level, step in enumerate(STEPS):
            count = rows // step
            pack[at : at + count, half(head)] = run[head, rows_of(off[head, level], rows, step), :].astype(BF16)
            at += count
    moves = [copy(pack, late.at[target], sems.at[target]) for target in range(4)]
    for moved in moves:
        moved.wait()


def project_kernel(marks, own, e1, e2, e3, late, w, send, keep, e0, wide, whole, weight, sems):
    rows, width = keep.shape
    part = rows // 4
    most = 3 * part
    place = lax.axis_index("head")
    chip, core = lax.div(place, 2), lax.rem(place, 2)
    column = pl.multiple_of(2 * chip * width, width)
    loads = [
        copy(own.at[pl.ds(0, most), :], e0, sems.at[0]),
        copy(w.at[:, pl.ds(column, 2 * width)], weight, sems.at[1]),
    ]
    for shift, pack in ((1, e1), (2, e2), (3, e3), (0, e0)):
        group = lax.rem(chip + 4 - shift, 4)
        if shift == 0:
            for moved in loads:
                moved.wait()
        for head in range(2):
            slot = 2 * shift + head
            first = marks[shift, 0, head]
            for turn in range(3):
                block = pl.multiple_of(lax.rem(first + turn + 1, 4) * part, part)
                whole[pl.ds(block, part), half(slot)] = pack[turn * part : (turn + 1) * part, half(head)]
            whole[pl.ds(pl.multiple_of(first * part, part), part), half(slot)] = late[group, :part, half(head)]
            at = part
            for level in (1, 2):
                step = STEPS[level] // 4
                count = part // step
                mark = marks[shift, level, head]
                block = pl.multiple_of(lax.rem(mark, 4) * part, part)
                held = 2 * slot + level - 1
                wide[held] = whole[pl.ds(block, part), half(slot)].astype(F32)
                wide[held, pl.ds(lax.div(mark, 4), count, stride=step), :] = late[
                    group, at : at + count, half(head)
                ].astype(F32)
                whole[pl.ds(block, part), half(slot)] = wide[held].astype(BF16)
                at += count

    def product(which):
        total = 0.0
        for shift, pack in enumerate((None, e1, e2, e3)):
            if shift:
                chosen = pack[pl.ds(pl.multiple_of(most + 16 + which * width, 16), width), :]
            else:
                chosen = weight[:, pl.ds(pl.multiple_of(which * width, width), width)]
            total = total + jnp.dot(
                whole[:, shift * width : (shift + 1) * width], chosen, preferred_element_type=F32
            )
        return total

    send[...] = product(1 - core).astype(BF16)
    keep[...] = product(core)


def finish_kernel(keep, other, out, wide):
    part = keep.shape[0] // 4
    for head in range(2):
        for turn in range(4):
            block = slice(turn * part, (turn + 1) * part)
            wide[head, pl.ds(turn, part, stride=4), :] = keep[block, half(head)] + other[block, half(head)].astype(F32)
        out[:, half(head)] = wide[head].astype(BF16)


def shards(queries, keys, values, offsets, w_out):
    rows, width = queries.shape
    spread, heads = lax.axis_size("seq"), lax.axis_size("head")
    lines = spread // 4
    along_y = [[4 * line + y for y in range(4)] for line in range(lines)]
    far_lines = [[(4 * b + line) * 4 + y for b in range(4)] for line in range(4) for y in range(4)]
    along_x = [[2 * chip + core for chip in range(4)] for core in range(2)]
    dma = pltpu.SemaphoreType.DMA

    def swap(value, axis, groups):
        return lax.all_to_all(value, axis, 0, 0, axis_index_groups=groups)

    def shift_z(value, by):
        hops = [(4 * (4 * b + z) + y, 4 * (4 * b + (z + by) % 4) + y) for b in range(lines // 4) for z in range(4) for y in range(4)]
        return lax.ppermute(value, "seq", hops)

    def shift_x(value, by):
        return lax.ppermute(value, "head", [(place, (place + 2 * by) % heads) for place in range(heads)])

    count = [rows // step for step in STEPS]
    late_rows = sum(count)
    near_rows = 2 * count[0] + count[1] + count[2]
    z_rows = 2 * count[1] + 2 * count[2]
    queries, keys, values, offsets, w_out = map(stay, (queries, keys, values, offsets, w_out))
    near, near_z, own_q = call(
        pick_kernel,
        (pltpu.HBM((4, near_rows, width), BF16), pltpu.HBM((z_rows, width), BF16), pltpu.HBM((count[0], width), BF16)),
        [HBM] * 4,
        (HBM,) * 3,
        [
            pltpu.SMEM((2, 3), jnp.int32),
            pltpu.VMEM((3, rows, width), BF16),
            pltpu.VMEM((3, 2, rows, HEAD_DIM), F32),
            pltpu.VMEM((near_rows, width), BF16),
            pltpu.VMEM((z_rows, width), BF16),
            pltpu.VMEM((count[0], width), BF16),
            dma((13,)),
        ],
    )(offsets, queries, keys, values)
    zs = [stay(part) for part in [near_z] + [shift_z(near_z, by) for by in (1, 2, 3)]]
    near = swap(near, "seq", along_y)
    most = 3 * rows // 4
    packed = pltpu.HBM((most + 16 + 2 * width, width), BF16)
    kept = pltpu.HBM((2, late_rows, HEAD_DIM), F32)
    early, *packs, mixed, logs = call(
        local_kernel,
        (pltpu.HBM((most + 16, width), BF16), packed, packed, packed, kept, kept),
        [HBM] * 5,
        (HBM,) * 6,
        [
            pltpu.SMEM((2, 3), jnp.int32),
            pltpu.VMEM((2, 3, rows, HEAD_DIM), BF16),
            pltpu.VMEM((2, 2, rows, HEAD_DIM), F32),
            pltpu.VMEM((most + 16, width), BF16),
            pltpu.VMEM((2, late_rows, HEAD_DIM), F32),
            pltpu.VMEM((2, late_rows, HEAD_DIM), F32),
            pltpu.VMEM(w_out.shape, BF16),
            dma((26,)),
        ],
    )(offsets, queries, keys, values, w_out)
    far_z = call(
        relay_kernel, pltpu.HBM((4, 4, 2 * count[2], width), BF16), [ANY] * 4 + [HBM, ANY], HBM, [pltpu.VMEM((4, 2 * count[2], width), BF16), dma((8,))]
    )(*zs, stay(early), near)
    far_z = swap(far_z, "seq", far_lines)
    packs = [shift_x(pack, by) for by, pack in enumerate(packs, 1)]
    marks = jnp.stack([part[most : most + 3, ::HEAD_DIM] for part in [early] + packs]).astype(jnp.int32)
    mixed, logs = call(
        near_kernel,
        (kept, kept),
        [HBM] * 2 + [ANY] + [HBM] * 2,
        (HBM,) * 2,
        [
            pltpu.SMEM((2, 3), jnp.int32),
            pltpu.VMEM((count[0], width), BF16),
            pltpu.VMEM((4, 2 * count[0], width), BF16),
            pltpu.VMEM(mixed.shape, F32),
            pltpu.VMEM(mixed.shape, F32),
            pltpu.VMEM((2, rows, HEAD_DIM), F32),
            pltpu.VMEM((2, rows, HEAD_DIM), F32),
            dma((5,)),
        ],
    )(offsets, stay(own_q), near, stay(mixed), stay(logs))
    back = call(
        far_kernel,
        pltpu.HBM((4, count[1] + count[2], 3 * HEAD_DIM), BF16),
        [ANY] * 5 + [VMEM, HBM],
        HBM,
        [
            pltpu.VMEM((4, count[1] + count[2], width), BF16),
            pltpu.VMEM((4, 2 * count[1], width), BF16),
            pltpu.VMEM((4, count[1] + count[2], 3 * HEAD_DIM), BF16),
            dma((7,)),
        ],
    )(near, *zs, far_z, stay(mixed))
    back = swap(back, "seq", along_y)
    late = call(
        merge_kernel,
        pltpu.HBM((4, late_rows, width), BF16),
        [HBM] * 3 + [VMEM] + [ANY] * 0,
        HBM,
        [
            pltpu.SMEM((2, 3), jnp.int32),
            pltpu.VMEM(mixed.shape, F32),
            pltpu.VMEM(mixed.shape, F32),
            pltpu.VMEM((2, rows, HEAD_DIM), F32),
            pltpu.VMEM((2, rows, HEAD_DIM), F32),
            pltpu.VMEM((late_rows, width), BF16),
            dma((4,)),
        ],
    )(offsets, stay(mixed), stay(logs), back)
    late = swap(late, "head", along_x)
    send, keep = call(
        project_kernel,
        (shape((rows, width), BF16), shape((rows, width), F32)),
        [SMEM, HBM] + [VMEM] * 4 + [HBM],
        (VMEM,) * 2,
        [
            pltpu.VMEM((most, width), BF16),
            pltpu.VMEM((16, count[0], HEAD_DIM), F32),
            pltpu.VMEM((rows, 4 * width), BF16),
            pltpu.VMEM((width, 2 * width), BF16),
            dma((2,)),
        ],
    )(marks, stay(early), *packs, late, w_out)
    other = lax.ppermute(send, "head", [(place, place ^ 1) for place in range(heads)])
    return call(
        finish_kernel,
        shape((rows, width), BF16),
        [VMEM] * 2,
        VMEM,
        [pltpu.VMEM((2, rows, HEAD_DIM), F32)],
    )(keep, other)


def solution(mesh):
    in_specs = (
        P("seq", "head"),
        P("seq", "head"),
        P("seq", "head"),
        P("head", None),
        P("head", None),
    )
    out_specs = P("seq", "head")
    return jax.shard_map(shards, mesh=mesh, in_specs=in_specs, out_specs=out_specs, check_vma=False)
```

```python
import math

import jax
import jax.numpy as jnp
from jax import lax
from jax.experimental import pallas as pl
from jax.experimental.pallas import tpu as pltpu
from jax.sharding import PartitionSpec as P

HEAD_DIM = 128
SCALE = HEAD_DIM ** (-0.5)
SCALE2 = SCALE * math.log2(math.e)
NEG = -1e30
F32 = jnp.float32
BF16 = jnp.bfloat16
STEPS = (4, 16, 64)
VMEM = pl.BlockSpec(memory_space=pltpu.VMEM)
SMEM = pl.BlockSpec(memory_space=pltpu.SMEM)
HBM = pl.BlockSpec(memory_space=pltpu.HBM)
ANY = pl.BlockSpec(memory_space=pl.ANY)
PARAMS = pltpu.CompilerParams(vmem_limit_bytes=20 << 20)


def half(head):
    return slice(head * HEAD_DIM, (head + 1) * HEAD_DIM)


def rows_of(offset, total, step):
    return pl.ds(offset, total // step, stride=step)


def call(kernel, out, in_specs, out_specs, scratch=()):
    return pl.pallas_call(
        kernel,
        out_shape=out,
        in_specs=in_specs,
        out_specs=out_specs,
        scratch_shapes=scratch,
        compiler_params=PARAMS,
    )


def shape(dims, dtype):
    return jax.ShapeDtypeStruct(dims, dtype)


def stay(value):
    return pltpu.with_memory_space_constraint(value, pltpu.HBM)


def copy(source, target, sem):
    moved = pltpu.make_async_copy(source, target, sem)
    moved.start()
    return moved


def attend(queries, keys, values, kept):
    scores = lax.dot_general(queries, keys, (((1,), (1,)), ((), ())), preferred_element_type=F32)
    scores = jnp.where(kept, scores, NEG)
    top = jnp.max(scores, axis=-1, keepdims=True)
    weights = jnp.where(kept, jnp.exp2((scores - top) * SCALE2), 0.0)
    total = jnp.sum(weights, axis=-1, keepdims=True)
    some = total > 0.0
    safe = jnp.where(some, total, 1.0)
    out = jnp.dot(weights.astype(BF16), values, preferred_element_type=F32) / safe
    return out, jnp.where(some, top * SCALE + jnp.log(safe), NEG)


def pick_kernel(off_in, q, k, v, near_out, near_z, own_q, off, raw, wide, near, pack, query, sems):
    rows = q.shape[0]
    count = [rows // step for step in STEPS]
    first = copy(off_in, off, sems.at[0])
    loads = [copy(source, raw.at[slot], sems.at[1 + slot]) for slot, source in enumerate((k, v, q))]
    moves = []
    first.wait()
    for slot in range(3):
        loads[slot].wait()
        for head in range(2):
            wide[slot, head] = raw[slot, :, half(head)].astype(F32)
            picks = [
                wide[slot, head, rows_of(off[head, level], rows, step), :].astype(BF16)
                for level, step in enumerate(STEPS)
            ]
            if slot < 2:
                near[slot * count[0] : (slot + 1) * count[0], half(head)] = picks[0]
                pack[slot * count[1] : (slot + 1) * count[1], half(head)] = picks[1]
                at = 2 * count[1] + slot * count[2]
                pack[at : at + count[2], half(head)] = picks[2]
            else:
                query[:, half(head)] = picks[0]
                at = 2 * count[0]
                near[at : at + count[1], half(head)] = picks[1]
                near[at + count[1] : at + count[1] + count[2], half(head)] = picks[2]
        if slot == 1:
            moves = [copy(pack, near_z, sems.at[4])]
    moves.append(copy(query, own_q, sems.at[8]))
    moves += [copy(near, near_out.at[target], sems.at[9 + target]) for target in range(4)]
    for moved in moves:
        moved.wait()


def relay_kernel(z0, z1, z2, z3, _1, _2, far_z, middle, part, sems):
    line = lax.rem(lax.div(lax.axis_index("seq"), 4), 4)
    moves = []
    for shift, z in enumerate((z0, z1, z2, z3)):
        place = lax.rem(line + 4 - shift, 4)
        part[place] = z[128:160, :]
        moves.append(copy(z.at[pl.ds(0, 128), :], middle.at[place], sems.at[shift]))
    moves += [copy(part, far_z.at[target], sems.at[4 + target]) for target in range(far_z.shape[0])]
    for moved in moves:
        moved.wait()


def local_kernel(off_in, q, k, v, w, own, out1, out2, out3, mixed, logs, off, raw, wide, early, some, some_logs, held, sems):
    chip = lax.div(lax.axis_index("head"), 2)
    rows, width = q.shape
    block = 512
    part = rows // 4
    first_copy = copy(off_in, off, sems.at[0])
    loads = []
    for head in range(2):
        for slot, source in enumerate((q, k, v)):
            loads.append(copy(source.at[:, pl.ds(head * HEAD_DIM, HEAD_DIM)], raw.at[head, slot], sems.at[1 + 3 * head + slot]))
    column = copy(w, held, sems.at[7])
    row = lax.broadcasted_iota(jnp.int32, (block, block), 0)
    kept = lax.broadcasted_iota(jnp.int32, (block, block), 1) <= row
    line = lax.broadcasted_iota(jnp.int32, (16, HEAD_DIM), 0)
    moves = []
    first_copy.wait()
    for head in range(2):
        for moved in loads[3 * head : 3 * head + 3]:
            moved.wait()
        for first in range(0, rows, block):
            last = first + block
            query = raw[head, 0, first:last, :]
            pieces = [(first, last)] + ([(0, first)] if first else [])
            scores = [
                lax.dot_general(query, raw[head, 1, low:high, :], (((1,), (1,)), ((), ())), preferred_element_type=F32)
                for low, high in pieces
            ]
            scores[0] = jnp.where(kept, scores[0], NEG)
            top = jnp.max(scores[0], axis=-1, keepdims=True)
            for piece in scores[1:]:
                top = jnp.maximum(top, jnp.max(piece, axis=-1, keepdims=True))
            total, out = 0.0, 0.0
            for piece, (low, high) in zip(scores, pieces):
                weights = jnp.exp2((piece - top) * SCALE2)
                total = total + jnp.sum(weights, axis=-1, keepdims=True)
                out = out + jnp.dot(weights.astype(BF16), raw[head, 2, low:high, :], preferred_element_type=F32)
            wide[head, 0, first:last, :] = out / total
            wide[head, 1, first:last, :] = jnp.broadcast_to(top * SCALE + jnp.log(total), out.shape)
        for turn in range(3):
            where = rows_of(lax.rem(off[head, 0] + turn + 1, 4), rows, 4)
            early[turn * part : (turn + 1) * part, half(head)] = wide[head, 0, where, :].astype(BF16)
        marks = jnp.where(line == 0, off[head, 0], jnp.where(line == 1, off[head, 1], off[head, 2]))
        early[3 * part :, half(head)] = marks.astype(F32).astype(BF16)
        at = 0
        for level, step in enumerate(STEPS):
            count = rows // step
            where = rows_of(off[head, level], rows, step)
            some[head, at : at + count, :] = wide[head, 0, where, :]
            some_logs[head, at : at + count, :] = wide[head, 1, where, :]
            at += count
        lanes = pl.ds(head * HEAD_DIM, HEAD_DIM)
        for slot, target in enumerate((own, out1, out2, out3)):
            place = target.at[pl.ds(0, 3 * part + 16), lanes]
            moves.append(copy(early.at[:, lanes], place, sems.at[8 + 4 * head + slot]))
        moves.append(copy(some.at[head], mixed.at[head], sems.at[16 + 2 * head]))
        moves.append(copy(some_logs.at[head], logs.at[head], sems.at[17 + 2 * head]))
        if head == 0:
            column.wait()
            for shift, target in enumerate((out1, out2, out3), 1):
                for side in range(2):
                    place = pl.multiple_of((2 * lax.rem(chip + shift, 4) + side) * width, width)
                    at = 3 * part + 16 + side * width
                    sem = sems.at[18 + 2 * shift + side]
                    moves.append(copy(held.at[:, pl.ds(place, width)], target.at[pl.ds(at, width), :], sem))
    for moved in moves:
        moved.wait()


def merge(parts):
    top = parts[0][1]
    for _, log in parts[1:]:
        top = jnp.maximum(top, log)
    total, out = 0.0, 0.0
    for value, log in parts:
        share = jnp.exp(log - top)
        total = total + share
        out = out + share * value
    return out / total, top + jnp.log(total)


def spread_rows(off, head, packed, wide):
    rows, at = wide.shape[1], 0
    for level, step in enumerate(STEPS):
        count = rows // step
        wide[head, rows_of(off[head, level], rows, step), :] = packed[head, at : at + count, :]
        at += count


def gather_rows(off, head, wide, packed):
    rows, at = wide.shape[1], 0
    for level, step in enumerate(STEPS):
        count = rows // step
        packed[head, at : at + count, :] = wide[head, rows_of(off[head, level], rows, step), :].astype(packed.dtype)
        at += count


def near_kernel(
    off_in, own_q, near_in, m_in, l_in, m_out, l_out, off, queries, near, mixed, logs, run, run_logs, sems
):
    count = own_q.shape[0]
    rows = 4 * count
    places = ((off_in, off), (own_q, queries), (near_in.at[:, pl.ds(0, 2 * count), :], near), (m_in, mixed), (l_in, logs))
    loads = [copy(source, target, sems.at[slot]) for slot, (source, target) in enumerate(places)]
    for moved in loads:
        moved.wait()
    mine = lax.rem(lax.axis_index("seq"), 4)
    for head in range(2):
        keys = near[:, :count, half(head)].reshape(-1, HEAD_DIM)
        values = near[:, count:, half(head)].reshape(-1, HEAD_DIM)
        dims = (count, 4 * count)
        query = mine * count + lax.broadcasted_iota(jnp.int32, dims, 0)
        key = lax.broadcasted_iota(jnp.int32, dims, 1)
        out, log = attend(queries[:, half(head)], keys, values, key <= query)
        log = jnp.broadcast_to(log, out.shape)
        out, log = merge([(mixed[head, :count, :], logs[head, :count, :]), (out, log)])
        spread_rows(off, head, mixed, run)
        spread_rows(off, head, logs, run_logs)
        where = rows_of(off[head, 0], rows, 4)
        run[head, where, :] = out
        run_logs[head, where, :] = log
        gather_rows(off, head, run, mixed)
        gather_rows(off, head, run_logs, logs)
    moves = [copy(mixed, m_out, sems.at[0]), copy(logs, l_out, sems.at[1])]
    for moved in moves:
        moved.wait()


def far_kernel(near_in, middle, hi, _, back, near, zs, part, sems):
    seq = lax.axis_index("seq")
    mine, line = lax.rem(seq, 4), lax.div(seq, 4)
    loads = [copy(middle, zs, sems.at[2])]
    loads.append(copy(near_in.at[:, pl.ds(512, 80), :], near, sems.at[0]))
    for moved in loads:
        moved.wait()
    at = 0
    for level, count in ((1, 64), (2, 16)):
        place = lax.rem(line, 4) if level == 1 else line
        logs = []
        for head in range(2):
            queries = near[:, at : at + count, half(head)].reshape(-1, HEAD_DIM)
            if level == 1:
                keys = zs[:, :count, half(head)].reshape(-1, HEAD_DIM)
                values = zs[:, count:, half(head)].reshape(-1, HEAD_DIM)
            else:
                keys = hi[:, :, :count, half(head)].reshape(-1, HEAD_DIM)
                values = hi[:, :, count:, half(head)].reshape(-1, HEAD_DIM)
            dims = (4 * count, keys.shape[0])
            row = lax.broadcasted_iota(jnp.int32, dims, 0)
            query = place * 4 * count + row
            key = lax.broadcasted_iota(jnp.int32, dims, 1)
            key = (lax.div(key, count) * 4 + mine) * count + lax.rem(key, count)
            out, log = attend(queries, keys, values, key <= query)
            logs.append(log)
            part[:, at : at + count, half(head)] = out.reshape(4, count, HEAD_DIM).astype(BF16)
        lane = lax.broadcasted_iota(jnp.int32, (4 * count, HEAD_DIM), 1)
        left = jnp.where(lane < HEAD_DIM // 2, logs[0], logs[1])
        both = left.astype(BF16)
        for piece in range(1, 3):
            left = left - left.astype(BF16).astype(F32)
            both = jnp.where(lax.rem(lane, HEAD_DIM // 2) < 16 * piece, both, left.astype(BF16))
        part[:, at : at + count, 2 * HEAD_DIM :] = both.reshape(4, count, HEAD_DIM)
        at += count
    moves = [copy(part, back, sems.at[1])]
    for moved in moves:
        moved.wait()


def merge_kernel(off_in, m_in, l_in, back, late, off, mixed, logs, run, run_logs, pack, sems):
    rows = run.shape[1]
    places = ((off_in, off), (m_in, mixed), (l_in, logs))
    loads = [copy(source, target, sems.at[slot]) for slot, (source, target) in enumerate(places)]
    for moved in loads:
        moved.wait()
    for head in range(2):
        spread_rows(off, head, mixed, run)
        spread_rows(off, head, logs, run_logs)
        at = 0
        for level in (1, 2):
            count = rows // STEPS[level]
            where = rows_of(off[head, level], rows, STEPS[level])
            parts = [(run[head, where, :], run_logs[head, where, :])]
            for source in range(4):
                lane = head * (HEAD_DIM // 2)
                pieces = back[source, at : at + count, 2 * HEAD_DIM :].astype(F32)
                log = sum(pieces[:, lane + 16 * piece : lane + 16 * piece + 1] for piece in range(3))
                value = back[source, at : at + count, half(head)].astype(F32)
                parts.append((value, jnp.broadcast_to(log, (count, HEAD_DIM))))
            at += count
            out, log = merge(parts)
            run[head, where, :] = out
            run_logs[head, where, :] = log
        at = 0
        for level, step in enumerate(STEPS):
            count = rows // step
            pack[at : at + count, half(head)] = run[head, rows_of(off[head, level], rows, step), :].astype(BF16)
            at += count
    moves = [copy(pack, late.at[target], sems.at[target]) for target in range(4)]
    for moved in moves:
        moved.wait()


def project_kernel(marks, own, e1, e2, e3, late, w, send, whole, e0, wide, weight, sems):
    rows, width = send.shape
    part = rows // 4
    most = 3 * part
    place = lax.axis_index("head")
    chip, core = lax.div(place, 2), lax.rem(place, 2)
    column = pl.multiple_of(2 * chip * width, width)
    loads = [
        copy(own.at[pl.ds(0, most), :], e0, sems.at[0]),
        copy(w.at[:, pl.ds(column, 2 * width)], weight, sems.at[1]),
    ]
    for shift, pack in ((1, e1), (2, e2), (3, e3), (0, e0)):
        group = lax.rem(chip + 4 - shift, 4)
        if shift == 0:
            for moved in loads:
                moved.wait()
        for head in range(2):
            slot = 2 * shift + head
            first = marks[shift, 0, head]
            for turn in range(3):
                block = pl.multiple_of(lax.rem(first + turn + 1, 4) * part, part)
                whole[pl.ds(block, part), half(slot)] = pack[turn * part : (turn + 1) * part, half(head)]
            whole[pl.ds(pl.multiple_of(first * part, part), part), half(slot)] = late[group, :part, half(head)]
            at = part
            for level in (1, 2):
                step = STEPS[level] // 4
                count = part // step
                mark = marks[shift, level, head]
                block = pl.multiple_of(lax.rem(mark, 4) * part, part)
                held = 2 * slot + level - 1
                wide[held] = whole[pl.ds(block, part), half(slot)].astype(F32)
                wide[held, pl.ds(lax.div(mark, 4), count, stride=step), :] = late[
                    group, at : at + count, half(head)
                ].astype(F32)
                whole[pl.ds(block, part), half(slot)] = wide[held].astype(BF16)
                at += count

    send[...] = product(whole, (e1, e2, e3), weight, 1 - core).astype(BF16)


def product(whole, packs, weight, which):
    rows, width = whole.shape[0], weight.shape[0]
    first = weight[:, pl.ds(pl.multiple_of(which * width, width), width)]
    total = jnp.dot(whole[:, :width], first, preferred_element_type=F32)
    for shift, pack in enumerate(packs, 1):
        chosen = pack[pl.ds(pl.multiple_of(3 * rows // 4 + 16 + which * width, 16), width), :]
        total = total + jnp.dot(whole[:, shift * width : (shift + 1) * width], chosen, preferred_element_type=F32)
    return total


def keep_kernel(whole, e1, e2, e3, w, keep, weight, sem):
    place = lax.axis_index("head")
    chip, core = lax.div(place, 2), lax.rem(place, 2)
    width = weight.shape[0]
    column = pl.multiple_of(2 * chip * width, width)
    copy(w.at[:, pl.ds(column, 2 * width)], weight, sem).wait()
    keep[...] = product(whole, (e1, e2, e3), weight, core)


def finish_kernel(keep, other, out, wide):
    part = keep.shape[0] // 4
    for head in range(2):
        for turn in range(4):
            block = slice(turn * part, (turn + 1) * part)
            wide[head, pl.ds(turn, part, stride=4), :] = keep[block, half(head)] + other[block, half(head)].astype(F32)
        out[:, half(head)] = wide[head].astype(BF16)


def shards(queries, keys, values, offsets, w_out):
    rows, width = queries.shape
    spread, heads = lax.axis_size("seq"), lax.axis_size("head")
    lines = spread // 4
    along_y = [[4 * line + y for y in range(4)] for line in range(lines)]
    far_lines = [[(4 * b + line) * 4 + y for b in range(4)] for line in range(4) for y in range(4)]
    along_x = [[2 * chip + core for chip in range(4)] for core in range(2)]
    dma = pltpu.SemaphoreType.DMA

    def swap(value, axis, groups):
        return lax.all_to_all(value, axis, 0, 0, axis_index_groups=groups)

    def shift_z(value, by):
        hops = [(4 * (4 * b + z) + y, 4 * (4 * b + (z + by) % 4) + y) for b in range(lines // 4) for z in range(4) for y in range(4)]
        return lax.ppermute(value, "seq", hops)

    def shift_x(value, by):
        return lax.ppermute(value, "head", [(place, (place + 2 * by) % heads) for place in range(heads)])

    count = [rows // step for step in STEPS]
    late_rows = sum(count)
    near_rows = 2 * count[0] + count[1] + count[2]
    z_rows = 2 * count[1] + 2 * count[2]
    queries, keys, values, offsets, w_out = map(stay, (queries, keys, values, offsets, w_out))
    near, near_z, own_q = call(
        pick_kernel,
        (pltpu.HBM((4, near_rows, width), BF16), pltpu.HBM((z_rows, width), BF16), pltpu.HBM((count[0], width), BF16)),
        [HBM] * 4,
        (HBM,) * 3,
        [
            pltpu.SMEM((2, 3), jnp.int32),
            pltpu.VMEM((3, rows, width), BF16),
            pltpu.VMEM((3, 2, rows, HEAD_DIM), F32),
            pltpu.VMEM((near_rows, width), BF16),
            pltpu.VMEM((z_rows, width), BF16),
            pltpu.VMEM((count[0], width), BF16),
            dma((13,)),
        ],
    )(offsets, queries, keys, values)
    zs = [near_z] + [shift_z(near_z, by) for by in (1, 2, 3)]
    near = swap(near, "seq", along_y)
    most = 3 * rows // 4
    packed = pltpu.HBM((most + 16 + 2 * width, width), BF16)
    kept = pltpu.HBM((2, late_rows, HEAD_DIM), F32)
    early, *packs, mixed, logs = call(
        local_kernel,
        (pltpu.HBM((most + 16, width), BF16), packed, packed, packed, kept, kept),
        [HBM] * 5,
        (HBM,) * 6,
        [
            pltpu.SMEM((2, 3), jnp.int32),
            pltpu.VMEM((2, 3, rows, HEAD_DIM), BF16),
            pltpu.VMEM((2, 2, rows, HEAD_DIM), F32),
            pltpu.VMEM((most + 16, width), BF16),
            pltpu.VMEM((2, late_rows, HEAD_DIM), F32),
            pltpu.VMEM((2, late_rows, HEAD_DIM), F32),
            pltpu.VMEM(w_out.shape, BF16),
            dma((26,)),
        ],
    )(offsets, queries, keys, values, w_out)
    far_z, middle = call(
        relay_kernel,
        (pltpu.HBM((4, 4, 2 * count[2], width), BF16), pltpu.HBM((4, 2 * count[1], width), BF16)),
        [VMEM] * 4 + [HBM, ANY],
        (HBM,) * 2,
        [pltpu.VMEM((4, 2 * count[2], width), BF16), dma((8,))],
    )(*zs, stay(early), near)
    far_z = swap(far_z, "seq", far_lines)
    packs = [shift_x(pack, by) for by, pack in enumerate(packs, 1)]
    marks = jnp.stack([part[most : most + 3, ::HEAD_DIM] for part in [early] + packs]).astype(jnp.int32)
    mixed, logs = call(
        near_kernel,
        (kept, kept),
        [HBM] * 2 + [ANY] + [HBM] * 2,
        (HBM,) * 2,
        [
            pltpu.SMEM((2, 3), jnp.int32),
            pltpu.VMEM((count[0], width), BF16),
            pltpu.VMEM((4, 2 * count[0], width), BF16),
            pltpu.VMEM(mixed.shape, F32),
            pltpu.VMEM(mixed.shape, F32),
            pltpu.VMEM((2, rows, HEAD_DIM), F32),
            pltpu.VMEM((2, rows, HEAD_DIM), F32),
            dma((5,)),
        ],
    )(offsets, stay(own_q), near, stay(mixed), stay(logs))
    back = call(
        far_kernel,
        pltpu.HBM((4, count[1] + count[2], 3 * HEAD_DIM), BF16),
        [ANY, HBM, VMEM, HBM],
        HBM,
        [
            pltpu.VMEM((4, count[1] + count[2], width), BF16),
            pltpu.VMEM((4, 2 * count[1], width), BF16),
            pltpu.VMEM((4, count[1] + count[2], 3 * HEAD_DIM), BF16),
            dma((7,)),
        ],
    )(near, stay(middle), far_z, stay(mixed))
    back = swap(back, "seq", along_y)
    late = call(
        merge_kernel,
        pltpu.HBM((4, late_rows, width), BF16),
        [HBM] * 3 + [VMEM] + [ANY] * 0,
        HBM,
        [
            pltpu.SMEM((2, 3), jnp.int32),
            pltpu.VMEM(mixed.shape, F32),
            pltpu.VMEM(mixed.shape, F32),
            pltpu.VMEM((2, rows, HEAD_DIM), F32),
            pltpu.VMEM((2, rows, HEAD_DIM), F32),
            pltpu.VMEM((late_rows, width), BF16),
            dma((4,)),
        ],
    )(offsets, stay(mixed), stay(logs), back)
    late = swap(late, "head", along_x)
    send, whole = call(
        project_kernel,
        (shape((rows, width), BF16), shape((rows, 4 * width), BF16)),
        [SMEM, HBM] + [VMEM] * 4 + [HBM],
        (VMEM,) * 2,
        [
            pltpu.VMEM((most, width), BF16),
            pltpu.VMEM((16, count[0], HEAD_DIM), F32),
            pltpu.VMEM((width, 2 * width), BF16),
            dma((2,)),
        ],
    )(marks, stay(early), *packs, late, w_out)
    keep = call(
        keep_kernel,
        shape((rows, width), F32),
        [VMEM] * 4 + [HBM],
        VMEM,
        [pltpu.VMEM((width, 2 * width), BF16), dma(())],
    )(whole, *packs, w_out)
    other = lax.ppermute(send, "head", [(place, place ^ 1) for place in range(heads)])
    return call(
        finish_kernel,
        shape((rows, width), BF16),
        [VMEM] * 2,
        VMEM,
        [pltpu.VMEM((2, rows, HEAD_DIM), F32)],
    )(keep, other)


def solution(mesh):
    in_specs = (
        P("seq", "head"),
        P("seq", "head"),
        P("seq", "head"),
        P("head", None),
        P("head", None),
    )
    out_specs = P("seq", "head")
    return jax.shard_map(shards, mesh=mesh, in_specs=in_specs, out_specs=out_specs, check_vma=False)
```

```python
import math

import jax
import jax.numpy as jnp
from jax import lax
from jax.experimental import pallas as pl
from jax.experimental.pallas import tpu as pltpu
from jax.sharding import PartitionSpec as P

HEAD_DIM = 128
SCALE = HEAD_DIM ** (-0.5)
SCALE2 = SCALE * math.log2(math.e)
NEG = -1e30
F32 = jnp.float32
BF16 = jnp.bfloat16
STEPS = (4, 16, 64)
VMEM = pl.BlockSpec(memory_space=pltpu.VMEM)
SMEM = pl.BlockSpec(memory_space=pltpu.SMEM)
HBM = pl.BlockSpec(memory_space=pltpu.HBM)
ANY = pl.BlockSpec(memory_space=pl.ANY)
PARAMS = pltpu.CompilerParams(vmem_limit_bytes=20 << 20)


def half(head):
    return slice(head * HEAD_DIM, (head + 1) * HEAD_DIM)


def rows_of(offset, total, step):
    return pl.ds(offset, total // step, stride=step)


def call(kernel, out, in_specs, out_specs, scratch=()):
    return pl.pallas_call(
        kernel,
        out_shape=out,
        in_specs=in_specs,
        out_specs=out_specs,
        scratch_shapes=scratch,
        compiler_params=PARAMS,
    )


def shape(dims, dtype):
    return jax.ShapeDtypeStruct(dims, dtype)


def stay(value):
    return pltpu.with_memory_space_constraint(value, pltpu.HBM)


def copy(source, target, sem):
    moved = pltpu.make_async_copy(source, target, sem)
    moved.start()
    return moved


def attend(queries, keys, values, kept):
    scores = lax.dot_general(queries, keys, (((1,), (1,)), ((), ())), preferred_element_type=F32)
    scores = jnp.where(kept, scores, NEG)
    top = jnp.max(scores, axis=-1, keepdims=True)
    weights = jnp.where(kept, jnp.exp2((scores - top) * SCALE2), 0.0)
    total = jnp.sum(weights, axis=-1, keepdims=True)
    some = total > 0.0
    safe = jnp.where(some, total, 1.0)
    out = jnp.dot(weights.astype(BF16), values, preferred_element_type=F32) / safe
    return out, jnp.where(some, top * SCALE + jnp.log(safe), NEG)


def pick_kernel(off_in, q, k, v, near_out, near_z, own_q, off, raw, wide, near, pack, query, sems):
    rows = q.shape[0]
    count = [rows // step for step in STEPS]
    first = copy(off_in, off, sems.at[0])
    loads = [copy(source, raw.at[slot], sems.at[1 + slot]) for slot, source in enumerate((k, v, q))]
    moves = []
    cuts = (0, count[0], 2 * count[0], near.shape[0])
    first.wait()
    for slot in range(3):
        loads[slot].wait()
        for head in range(2):
            wide[slot, head] = raw[slot, :, half(head)].astype(F32)
            picks = [
                wide[slot, head, rows_of(off[head, level], rows, step), :].astype(BF16)
                for level, step in enumerate(STEPS)
            ]
            if slot < 2:
                near[slot * count[0] : (slot + 1) * count[0], half(head)] = picks[0]
                pack[slot * count[1] : (slot + 1) * count[1], half(head)] = picks[1]
                at = 2 * count[1] + slot * count[2]
                pack[at : at + count[2], half(head)] = picks[2]
            else:
                query[:, half(head)] = picks[0]
                at = 2 * count[0]
                near[at : at + count[1], half(head)] = picks[1]
                near[at + count[1] : at + count[1] + count[2], half(head)] = picks[2]
        piece = pl.ds(cuts[slot], cuts[slot + 1] - cuts[slot])
        for target in range(4):
            moves.append(copy(near.at[piece, :], near_out.at[target, piece, :], sems.at[9 + 4 * slot + target]))
        if slot == 1:
            moves.append(copy(pack, near_z, sems.at[4]))
    moves.append(copy(query, own_q, sems.at[8]))
    for moved in moves:
        moved.wait()


def relay_kernel(z0, z1, z2, z3, _1, _2, far_z, middle, part, sems):
    line = lax.rem(lax.div(lax.axis_index("seq"), 4), 4)
    moves = []
    for shift, z in enumerate((z0, z1, z2, z3)):
        place = lax.rem(line + 4 - shift, 4)
        part[place] = z[128:160, :]
        moves.append(copy(z.at[pl.ds(0, 128), :], middle.at[place], sems.at[shift]))
    moves += [copy(part, far_z.at[target], sems.at[4 + target]) for target in range(far_z.shape[0])]
    for moved in moves:
        moved.wait()


def local_kernel(off_in, q, k, v, w, own, out1, out2, out3, mixed, logs, off, raw, wide, early, some, some_logs, held, sems):
    chip = lax.div(lax.axis_index("head"), 2)
    rows, width = q.shape
    block = 512
    part = rows // 4
    first_copy = copy(off_in, off, sems.at[0])
    loads = []
    for head in range(2):
        for slot, source in enumerate((q, k, v)):
            loads.append(copy(source.at[:, pl.ds(head * HEAD_DIM, HEAD_DIM)], raw.at[head, slot], sems.at[1 + 3 * head + slot]))
    column = copy(w, held, sems.at[7])
    row = lax.broadcasted_iota(jnp.int32, (block, block), 0)
    kept = lax.broadcasted_iota(jnp.int32, (block, block), 1) <= row
    line = lax.broadcasted_iota(jnp.int32, (16, HEAD_DIM), 0)
    moves = []
    first_copy.wait()
    for head in range(2):
        for moved in loads[3 * head : 3 * head + 3]:
            moved.wait()
        for first in range(0, rows, block):
            last = first + block
            query = raw[head, 0, first:last, :]
            pieces = [(first, last)] + ([(0, first)] if first else [])
            scores = [
                lax.dot_general(query, raw[head, 1, low:high, :], (((1,), (1,)), ((), ())), preferred_element_type=F32)
                for low, high in pieces
            ]
            scores[0] = jnp.where(kept, scores[0], NEG)
            top = jnp.max(scores[0], axis=-1, keepdims=True)
            for piece in scores[1:]:
                top = jnp.maximum(top, jnp.max(piece, axis=-1, keepdims=True))
            total, out = 0.0, 0.0
            for piece, (low, high) in zip(scores, pieces):
                weights = jnp.exp2((piece - top) * SCALE2)
                total = total + jnp.sum(weights, axis=-1, keepdims=True)
                out = out + jnp.dot(weights.astype(BF16), raw[head, 2, low:high, :], preferred_element_type=F32)
            wide[head, 0, first:last, :] = out / total
            wide[head, 1, first:last, :] = jnp.broadcast_to(top * SCALE + jnp.log(total), out.shape)
        for turn in range(3):
            where = rows_of(lax.rem(off[head, 0] + turn + 1, 4), rows, 4)
            early[turn * part : (turn + 1) * part, half(head)] = wide[head, 0, where, :].astype(BF16)
        marks = jnp.where(line == 0, off[head, 0], jnp.where(line == 1, off[head, 1], off[head, 2]))
        early[3 * part :, half(head)] = marks.astype(F32).astype(BF16)
        at = 0
        for level, step in enumerate(STEPS):
            count = rows // step
            where = rows_of(off[head, level], rows, step)
            some[head, at : at + count, :] = wide[head, 0, where, :]
            some_logs[head, at : at + count, :] = wide[head, 1, where, :]
            at += count
        lanes = pl.ds(head * HEAD_DIM, HEAD_DIM)
        for slot, target in enumerate((own, out1, out2, out3)):
            place = target.at[pl.ds(0, 3 * part + 16), lanes]
            moves.append(copy(early.at[:, lanes], place, sems.at[8 + 4 * head + slot]))
        moves.append(copy(some.at[head], mixed.at[head], sems.at[16 + 2 * head]))
        moves.append(copy(some_logs.at[head], logs.at[head], sems.at[17 + 2 * head]))
        if head == 0:
            column.wait()
            for shift, target in enumerate((out1, out2, out3), 1):
                for side in range(2):
                    place = pl.multiple_of((2 * lax.rem(chip + shift, 4) + side) * width, width)
                    at = 3 * part + 16 + side * width
                    sem = sems.at[18 + 2 * shift + side]
                    moves.append(copy(held.at[:, pl.ds(place, width)], target.at[pl.ds(at, width), :], sem))
    for moved in moves:
        moved.wait()


def merge(parts):
    top = parts[0][1]
    for _, log in parts[1:]:
        top = jnp.maximum(top, log)
    total, out = 0.0, 0.0
    for value, log in parts:
        share = jnp.exp(log - top)
        total = total + share
        out = out + share * value
    return out / total, top + jnp.log(total)


def spread_rows(off, head, packed, wide):
    rows, at = wide.shape[1], 0
    for level, step in enumerate(STEPS):
        count = rows // step
        wide[head, rows_of(off[head, level], rows, step), :] = packed[head, at : at + count, :]
        at += count


def gather_rows(off, head, wide, packed):
    rows, at = wide.shape[1], 0
    for level, step in enumerate(STEPS):
        count = rows // step
        packed[head, at : at + count, :] = wide[head, rows_of(off[head, level], rows, step), :].astype(packed.dtype)
        at += count


def near_kernel(
    off_in, own_q, near_in, m_in, l_in, m_out, l_out, off, queries, near, mixed, logs, run, run_logs, sems
):
    count = own_q.shape[0]
    rows = 4 * count
    places = ((off_in, off), (own_q, queries), (near_in.at[:, pl.ds(0, 2 * count), :], near), (m_in, mixed), (l_in, logs))
    loads = [copy(source, target, sems.at[slot]) for slot, (source, target) in enumerate(places)]
    for moved in loads:
        moved.wait()
    mine = lax.rem(lax.axis_index("seq"), 4)
    for head in range(2):
        keys = near[:, :count, half(head)].reshape(-1, HEAD_DIM)
        values = near[:, count:, half(head)].reshape(-1, HEAD_DIM)
        dims = (count, 4 * count)
        query = mine * count + lax.broadcasted_iota(jnp.int32, dims, 0)
        key = lax.broadcasted_iota(jnp.int32, dims, 1)
        out, log = attend(queries[:, half(head)], keys, values, key <= query)
        log = jnp.broadcast_to(log, out.shape)
        out, log = merge([(mixed[head, :count, :], logs[head, :count, :]), (out, log)])
        spread_rows(off, head, mixed, run)
        spread_rows(off, head, logs, run_logs)
        where = rows_of(off[head, 0], rows, 4)
        run[head, where, :] = out
        run_logs[head, where, :] = log
        gather_rows(off, head, run, mixed)
        gather_rows(off, head, run_logs, logs)
    moves = [copy(mixed, m_out, sems.at[0]), copy(logs, l_out, sems.at[1])]
    for moved in moves:
        moved.wait()


def far_kernel(near, middle, hi, _, back, zs, part, sems):
    seq = lax.axis_index("seq")
    mine, line = lax.rem(seq, 4), lax.div(seq, 4)
    skip = near.shape[1] - part.shape[1]
    held = copy(middle, zs, sems.at[0])
    for level, count, at in ((2, 16, 64), (1, 64, 0)):
        if level == 1:
            held.wait()
        place = lax.rem(line, 4) if level == 1 else line
        logs = []
        for head in range(2):
            queries = near[:, skip + at : skip + at + count, half(head)].reshape(-1, HEAD_DIM)
            if level == 1:
                keys = zs[:, :count, half(head)].reshape(-1, HEAD_DIM)
                values = zs[:, count:, half(head)].reshape(-1, HEAD_DIM)
            else:
                keys = hi[:, :, :count, half(head)].reshape(-1, HEAD_DIM)
                values = hi[:, :, count:, half(head)].reshape(-1, HEAD_DIM)
            dims = (4 * count, keys.shape[0])
            row = lax.broadcasted_iota(jnp.int32, dims, 0)
            query = place * 4 * count + row
            key = lax.broadcasted_iota(jnp.int32, dims, 1)
            key = (lax.div(key, count) * 4 + mine) * count + lax.rem(key, count)
            out, log = attend(queries, keys, values, key <= query)
            logs.append(log)
            part[:, at : at + count, half(head)] = out.reshape(4, count, HEAD_DIM).astype(BF16)
        lane = lax.broadcasted_iota(jnp.int32, (4 * count, HEAD_DIM), 1)
        left = jnp.where(lane < HEAD_DIM // 2, logs[0], logs[1])
        both = left.astype(BF16)
        for piece in range(1, 3):
            left = left - left.astype(BF16).astype(F32)
            both = jnp.where(lax.rem(lane, HEAD_DIM // 2) < 16 * piece, both, left.astype(BF16))
        part[:, at : at + count, 2 * HEAD_DIM :] = both.reshape(4, count, HEAD_DIM)
    moves = [copy(part, back, sems.at[1])]
    for moved in moves:
        moved.wait()


def merge_kernel(off, mixed, logs, back, late, run, run_logs, pack, sems):
    rows = run.shape[1]
    for head in range(2):
        spread_rows(off, head, mixed, run)
        spread_rows(off, head, logs, run_logs)
        at = 0
        for level in (1, 2):
            count = rows // STEPS[level]
            where = rows_of(off[head, level], rows, STEPS[level])
            parts = [(run[head, where, :], run_logs[head, where, :])]
            for source in range(4):
                lane = head * (HEAD_DIM // 2)
                pieces = back[source, at : at + count, 2 * HEAD_DIM :].astype(F32)
                log = sum(pieces[:, lane + 16 * piece : lane + 16 * piece + 1] for piece in range(3))
                value = back[source, at : at + count, half(head)].astype(F32)
                parts.append((value, jnp.broadcast_to(log, (count, HEAD_DIM))))
            at += count
            out, log = merge(parts)
            run[head, where, :] = out
            run_logs[head, where, :] = log
        at = 0
        for level, step in enumerate(STEPS):
            count = rows // step
            pack[at : at + count, half(head)] = run[head, rows_of(off[head, level], rows, step), :].astype(BF16)
            at += count
    moves = [copy(pack, late.at[target], sems.at[target]) for target in range(4)]
    for moved in moves:
        moved.wait()


def project_kernel(marks, own, e1, e2, e3, late, w, send, whole, e0, wide, weight, sems):
    rows, width = send.shape
    part = rows // 4
    most = 3 * part
    place = lax.axis_index("head")
    chip, core = lax.div(place, 2), lax.rem(place, 2)
    column = pl.multiple_of(2 * chip * width, width)
    loads = [
        copy(own.at[pl.ds(0, most), :], e0, sems.at[0]),
        copy(w.at[:, pl.ds(column, 2 * width)], weight, sems.at[1]),
    ]
    for shift, pack in ((1, e1), (2, e2), (3, e3), (0, e0)):
        group = lax.rem(chip + 4 - shift, 4)
        if shift == 0:
            for moved in loads:
                moved.wait()
        for head in range(2):
            slot = 2 * shift + head
            first = marks[shift, 0, head]
            for turn in range(3):
                block = pl.multiple_of(lax.rem(first + turn + 1, 4) * part, part)
                whole[pl.ds(block, part), half(slot)] = pack[turn * part : (turn + 1) * part, half(head)]
            whole[pl.ds(pl.multiple_of(first * part, part), part), half(slot)] = late[group, :part, half(head)]
            at = part
            for level in (1, 2):
                step = STEPS[level] // 4
                count = part // step
                mark = marks[shift, level, head]
                block = pl.multiple_of(lax.rem(mark, 4) * part, part)
                held = 2 * slot + level - 1
                wide[held] = whole[pl.ds(block, part), half(slot)].astype(F32)
                wide[held, pl.ds(lax.div(mark, 4), count, stride=step), :] = late[
                    group, at : at + count, half(head)
                ].astype(F32)
                whole[pl.ds(block, part), half(slot)] = wide[held].astype(BF16)
                at += count

    send[...] = product(whole, (e1, e2, e3), weight, 1 - core).astype(BF16)


def product(whole, packs, weight, which):
    rows, width = whole.shape[0], weight.shape[0]
    first = weight[:, pl.ds(pl.multiple_of(which * width, width), width)]
    total = jnp.dot(whole[:, :width], first, preferred_element_type=F32)
    for shift, pack in enumerate(packs, 1):
        chosen = pack[pl.ds(pl.multiple_of(3 * rows // 4 + 16 + which * width, 16), width), :]
        total = total + jnp.dot(whole[:, shift * width : (shift + 1) * width], chosen, preferred_element_type=F32)
    return total


def keep_kernel(whole, e1, e2, e3, w, keep, weight, sem):
    place = lax.axis_index("head")
    chip, core = lax.div(place, 2), lax.rem(place, 2)
    width = weight.shape[0]
    column = pl.multiple_of(2 * chip * width, width)
    copy(w.at[:, pl.ds(column, 2 * width)], weight, sem).wait()
    keep[...] = product(whole, (e1, e2, e3), weight, core)


def finish_kernel(keep, other, out, wide):
    part = keep.shape[0] // 4
    for head in range(2):
        for turn in range(4):
            block = slice(turn * part, (turn + 1) * part)
            wide[head, pl.ds(turn, part, stride=4), :] = keep[block, half(head)] + other[block, half(head)].astype(F32)
        out[:, half(head)] = wide[head].astype(BF16)


def shards(queries, keys, values, offsets, w_out):
    rows, width = queries.shape
    spread, heads = lax.axis_size("seq"), lax.axis_size("head")
    lines = spread // 4
    along_y = [[4 * line + y for y in range(4)] for line in range(lines)]
    far_lines = [[(4 * b + line) * 4 + y for b in range(4)] for line in range(4) for y in range(4)]
    along_x = [[2 * chip + core for chip in range(4)] for core in range(2)]
    dma = pltpu.SemaphoreType.DMA

    def swap(value, axis, groups):
        return lax.all_to_all(value, axis, 0, 0, axis_index_groups=groups)

    def shift_z(value, by):
        hops = [(4 * (4 * b + z) + y, 4 * (4 * b + (z + by) % 4) + y) for b in range(lines // 4) for z in range(4) for y in range(4)]
        return lax.ppermute(value, "seq", hops)

    def shift_x(value, by):
        return lax.ppermute(value, "head", [(place, (place + 2 * by) % heads) for place in range(heads)])

    count = [rows // step for step in STEPS]
    late_rows = sum(count)
    near_rows = 2 * count[0] + count[1] + count[2]
    z_rows = 2 * count[1] + 2 * count[2]
    raw_offsets = offsets
    queries, keys, values, offsets, w_out = map(stay, (queries, keys, values, offsets, w_out))
    near, near_z, own_q = call(
        pick_kernel,
        (pltpu.HBM((4, near_rows, width), BF16), pltpu.HBM((z_rows, width), BF16), pltpu.HBM((count[0], width), BF16)),
        [HBM] * 4,
        (HBM,) * 3,
        [
            pltpu.SMEM((2, 3), jnp.int32),
            pltpu.VMEM((3, rows, width), BF16),
            pltpu.VMEM((3, 2, rows, HEAD_DIM), F32),
            pltpu.VMEM((near_rows, width), BF16),
            pltpu.VMEM((z_rows, width), BF16),
            pltpu.VMEM((count[0], width), BF16),
            dma((21,)),
        ],
    )(offsets, queries, keys, values)
    zs = [near_z] + [shift_z(near_z, by) for by in (1, 2, 3)]
    near = swap(near, "seq", along_y)
    most = 3 * rows // 4
    packed = pltpu.HBM((most + 16 + 2 * width, width), BF16)
    kept = pltpu.HBM((2, late_rows, HEAD_DIM), F32)
    early, *packs, mixed, logs = call(
        local_kernel,
        (pltpu.HBM((most + 16, width), BF16), packed, packed, packed, kept, kept),
        [HBM] * 5,
        (HBM,) * 6,
        [
            pltpu.SMEM((2, 3), jnp.int32),
            pltpu.VMEM((2, 3, rows, HEAD_DIM), BF16),
            pltpu.VMEM((2, 2, rows, HEAD_DIM), F32),
            pltpu.VMEM((most + 16, width), BF16),
            pltpu.VMEM((2, late_rows, HEAD_DIM), F32),
            pltpu.VMEM((2, late_rows, HEAD_DIM), F32),
            pltpu.VMEM(w_out.shape, BF16),
            dma((26,)),
        ],
    )(offsets, queries, keys, values, w_out)
    far_z, middle = call(
        relay_kernel,
        (pltpu.HBM((4, 4, 2 * count[2], width), BF16), pltpu.HBM((4, 2 * count[1], width), BF16)),
        [VMEM] * 4 + [HBM, ANY],
        (HBM,) * 2,
        [pltpu.VMEM((4, 2 * count[2], width), BF16), dma((8,))],
    )(*zs, stay(early), near)
    far_z = swap(far_z, "seq", far_lines)
    packs = [shift_x(pack, by) for by, pack in enumerate(packs, 1)]
    marks = jnp.stack([part[most : most + 3, ::HEAD_DIM] for part in [early] + packs]).astype(jnp.int32)
    mixed, logs = call(
        near_kernel,
        (kept, kept),
        [HBM] * 2 + [ANY] + [HBM] * 2,
        (HBM,) * 2,
        [
            pltpu.SMEM((2, 3), jnp.int32),
            pltpu.VMEM((count[0], width), BF16),
            pltpu.VMEM((4, 2 * count[0], width), BF16),
            pltpu.VMEM(mixed.shape, F32),
            pltpu.VMEM(mixed.shape, F32),
            pltpu.VMEM((2, rows, HEAD_DIM), F32),
            pltpu.VMEM((2, rows, HEAD_DIM), F32),
            dma((5,)),
        ],
    )(offsets, stay(own_q), near, stay(mixed), stay(logs))
    back = call(
        far_kernel,
        pltpu.HBM((4, count[1] + count[2], 3 * HEAD_DIM), BF16),
        [VMEM, HBM, VMEM, HBM],
        HBM,
        [
            pltpu.VMEM((4, 2 * count[1], width), BF16),
            pltpu.VMEM((4, count[1] + count[2], 3 * HEAD_DIM), BF16),
            dma((2,)),
        ],
    )(near, stay(middle), far_z, stay(mixed))
    back = swap(back, "seq", along_y)
    late = call(
        merge_kernel,
        pltpu.HBM((4, late_rows, width), BF16),
        [SMEM] + [VMEM] * 3,
        HBM,
        [
            pltpu.VMEM((2, rows, HEAD_DIM), F32),
            pltpu.VMEM((2, rows, HEAD_DIM), F32),
            pltpu.VMEM((late_rows, width), BF16),
            dma((4,)),
        ],
    )(raw_offsets, mixed, logs, back)
    late = swap(late, "head", along_x)
    send, whole = call(
        project_kernel,
        (shape((rows, width), BF16), shape((rows, 4 * width), BF16)),
        [SMEM, HBM] + [VMEM] * 4 + [HBM],
        (VMEM,) * 2,
        [
            pltpu.VMEM((most, width), BF16),
            pltpu.VMEM((16, count[0], HEAD_DIM), F32),
            pltpu.VMEM((width, 2 * width), BF16),
            dma((2,)),
        ],
    )(marks, stay(early), *packs, late, w_out)
    keep = call(
        keep_kernel,
        shape((rows, width), F32),
        [VMEM] * 4 + [HBM],
        VMEM,
        [pltpu.VMEM((width, 2 * width), BF16), dma(())],
    )(whole, *packs, w_out)
    other = lax.ppermute(send, "head", [(place, place ^ 1) for place in range(heads)])
    return call(
        finish_kernel,
        shape((rows, width), BF16),
        [VMEM] * 2,
        VMEM,
        [pltpu.VMEM((2, rows, HEAD_DIM), F32)],
    )(keep, other)


def solution(mesh):
    in_specs = (
        P("seq", "head"),
        P("seq", "head"),
        P("seq", "head"),
        P("head", None),
        P("head", None),
    )
    out_specs = P("seq", "head")
    return jax.shard_map(shards, mesh=mesh, in_specs=in_specs, out_specs=out_specs, check_vma=False)
```

```python
import math

import jax
import jax.numpy as jnp
from jax import lax
from jax.experimental import pallas as pl
from jax.experimental.pallas import tpu as pltpu
from jax.sharding import PartitionSpec as P

HEAD_DIM = 128
SCALE = HEAD_DIM ** (-0.5)
SCALE2 = SCALE * math.log2(math.e)
NEG = -1e30
F32 = jnp.float32
BF16 = jnp.bfloat16
STEPS = (4, 16, 64)
VMEM = pl.BlockSpec(memory_space=pltpu.VMEM)
SMEM = pl.BlockSpec(memory_space=pltpu.SMEM)
HBM = pl.BlockSpec(memory_space=pltpu.HBM)
ANY = pl.BlockSpec(memory_space=pl.ANY)
PARAMS = pltpu.CompilerParams(vmem_limit_bytes=20 << 20)


def half(head):
    return slice(head * HEAD_DIM, (head + 1) * HEAD_DIM)


def rows_of(offset, total, step):
    return pl.ds(offset, total // step, stride=step)


def call(kernel, out, in_specs, out_specs, scratch=()):
    return pl.pallas_call(
        kernel,
        out_shape=out,
        in_specs=in_specs,
        out_specs=out_specs,
        scratch_shapes=scratch,
        compiler_params=PARAMS,
    )


def shape(dims, dtype):
    return jax.ShapeDtypeStruct(dims, dtype)


def stay(value):
    return pltpu.with_memory_space_constraint(value, pltpu.HBM)


def copy(source, target, sem):
    moved = pltpu.make_async_copy(source, target, sem)
    moved.start()
    return moved


def attend(queries, keys, values, kept):
    scores = lax.dot_general(queries, keys, (((1,), (1,)), ((), ())), preferred_element_type=F32)
    scores = jnp.where(kept, scores, NEG)
    top = jnp.max(scores, axis=-1, keepdims=True)
    weights = jnp.where(kept, jnp.exp2((scores - top) * SCALE2), 0.0)
    total = jnp.sum(weights, axis=-1, keepdims=True)
    some = total > 0.0
    safe = jnp.where(some, total, 1.0)
    out = jnp.dot(weights.astype(BF16), values, preferred_element_type=F32) / safe
    return out, jnp.where(some, top * SCALE + jnp.log(safe), NEG)


def pick_kernel(off_in, q, k, v, near_out, near_z, own_q, off, raw, wide, near, pack, query, sems):
    rows = q.shape[0]
    count = [rows // step for step in STEPS]
    first = copy(off_in, off, sems.at[0])
    loads = [copy(source, raw.at[slot], sems.at[1 + slot]) for slot, source in enumerate((k, v, q))]
    moves = []
    cuts = (0, count[0], 2 * count[0], near.shape[0])
    first.wait()
    for slot in range(3):
        loads[slot].wait()
        for head in range(2):
            wide[slot, head] = raw[slot, :, half(head)].astype(F32)
            picks = [
                wide[slot, head, rows_of(off[head, level], rows, step), :].astype(BF16)
                for level, step in enumerate(STEPS)
            ]
            if slot < 2:
                near[slot * count[0] : (slot + 1) * count[0], half(head)] = picks[0]
                pack[slot * count[1] : (slot + 1) * count[1], half(head)] = picks[1]
                at = 2 * count[1] + slot * count[2]
                pack[at : at + count[2], half(head)] = picks[2]
            else:
                query[:, half(head)] = picks[0]
                at = 2 * count[0]
                near[at : at + count[1], half(head)] = picks[1]
                near[at + count[1] : at + count[1] + count[2], half(head)] = picks[2]
        piece = pl.ds(cuts[slot], cuts[slot + 1] - cuts[slot])
        for target in range(4):
            moves.append(copy(near.at[piece, :], near_out.at[target, piece, :], sems.at[9 + 4 * slot + target]))
        if slot == 1:
            moves.append(copy(pack, near_z, sems.at[4]))
    moves.append(copy(query, own_q, sems.at[8]))
    for moved in moves:
        moved.wait()


def relay_kernel(z0, z1, z2, z3, _1, _2, far_z, middle, part, sems):
    line = lax.rem(lax.div(lax.axis_index("seq"), 4), 4)
    moves = []
    for shift, z in enumerate((z0, z1, z2, z3)):
        place = lax.rem(line + 4 - shift, 4)
        part[place] = z[128:160, :]
        moves.append(copy(z.at[pl.ds(0, 128), :], middle.at[place], sems.at[shift]))
    moves += [copy(part, far_z.at[target], sems.at[4 + target]) for target in range(far_z.shape[0])]
    for moved in moves:
        moved.wait()


def local_kernel(off_in, q, k, v, w, own, out1, out2, out3, mixed, logs, off, raw, wide, early, some, some_logs, held, sems):
    chip = lax.div(lax.axis_index("head"), 2)
    rows, width = q.shape
    block = 512
    part = rows // 4
    first_copy = copy(off_in, off, sems.at[0])
    loads = []
    for head in range(2):
        for slot, source in enumerate((q, k, v)):
            loads.append(copy(source.at[:, pl.ds(head * HEAD_DIM, HEAD_DIM)], raw.at[head, slot], sems.at[1 + 3 * head + slot]))
    column = copy(w, held, sems.at[7])
    row = lax.broadcasted_iota(jnp.int32, (block, block), 0)
    kept = lax.broadcasted_iota(jnp.int32, (block, block), 1) <= row
    line = lax.broadcasted_iota(jnp.int32, (16, HEAD_DIM), 0)
    moves = []
    first_copy.wait()
    for head in range(2):
        for moved in loads[3 * head : 3 * head + 3]:
            moved.wait()
        for first in range(0, rows, block):
            last = first + block
            query = raw[head, 0, first:last, :]
            pieces = [(first, last)] + ([(0, first)] if first else [])
            scores = [
                lax.dot_general(query, raw[head, 1, low:high, :], (((1,), (1,)), ((), ())), preferred_element_type=F32)
                for low, high in pieces
            ]
            scores[0] = jnp.where(kept, scores[0], NEG)
            top = jnp.max(scores[0], axis=-1, keepdims=True)
            for piece in scores[1:]:
                top = jnp.maximum(top, jnp.max(piece, axis=-1, keepdims=True))
            total, out = 0.0, 0.0
            for piece, (low, high) in zip(scores, pieces):
                weights = jnp.exp2((piece - top) * SCALE2)
                total = total + jnp.sum(weights, axis=-1, keepdims=True)
                out = out + jnp.dot(weights.astype(BF16), raw[head, 2, low:high, :], preferred_element_type=F32)
            wide[head, 0, first:last, :] = out / total
            wide[head, 1, first:last, :] = jnp.broadcast_to(top * SCALE + jnp.log(total), out.shape)
        for turn in range(3):
            where = rows_of(lax.rem(off[head, 0] + turn + 1, 4), rows, 4)
            early[turn * part : (turn + 1) * part, half(head)] = wide[head, 0, where, :].astype(BF16)
        marks = jnp.where(line == 0, off[head, 0], jnp.where(line == 1, off[head, 1], off[head, 2]))
        early[3 * part :, half(head)] = marks.astype(F32).astype(BF16)
        at = 0
        for level, step in enumerate(STEPS):
            count = rows // step
            where = rows_of(off[head, level], rows, step)
            some[head, at : at + count, :] = wide[head, 0, where, :]
            some_logs[head, at : at + count, :] = wide[head, 1, where, :]
            at += count
        lanes = pl.ds(head * HEAD_DIM, HEAD_DIM)
        for slot, target in enumerate((own, out1, out2, out3)):
            place = target.at[pl.ds(0, 3 * part + 16), lanes]
            moves.append(copy(early.at[:, lanes], place, sems.at[8 + 4 * head + slot]))
        moves.append(copy(some.at[head], mixed.at[head], sems.at[16 + 2 * head]))
        moves.append(copy(some_logs.at[head], logs.at[head], sems.at[17 + 2 * head]))
        if head == 0:
            column.wait()
            for shift, target in enumerate((out1, out2, out3), 1):
                for side in range(2):
                    place = pl.multiple_of((2 * lax.rem(chip + shift, 4) + side) * width, width)
                    at = 3 * part + 16 + side * width
                    sem = sems.at[18 + 2 * shift + side]
                    moves.append(copy(held.at[:, pl.ds(place, width)], target.at[pl.ds(at, width), :], sem))
    for moved in moves:
        moved.wait()


def merge(parts):
    top = parts[0][1]
    for _, log in parts[1:]:
        top = jnp.maximum(top, log)
    total, out = 0.0, 0.0
    for value, log in parts:
        share = jnp.exp(log - top)
        total = total + share
        out = out + share * value
    return out / total, top + jnp.log(total)


def spread_rows(off, head, packed, wide):
    rows, at = wide.shape[1], 0
    for level, step in enumerate(STEPS):
        count = rows // step
        wide[head, rows_of(off[head, level], rows, step), :] = packed[head, at : at + count, :]
        at += count


def gather_rows(off, head, wide, packed):
    rows, at = wide.shape[1], 0
    for level, step in enumerate(STEPS):
        count = rows // step
        packed[head, at : at + count, :] = wide[head, rows_of(off[head, level], rows, step), :].astype(packed.dtype)
        at += count


def near_kernel(
    off_in, own_q, near_in, m_in, l_in, m_out, l_out, off, queries, near, mixed, logs, run, run_logs, sems
):
    count = own_q.shape[0]
    rows = 4 * count
    places = ((off_in, off), (own_q, queries), (near_in.at[:, pl.ds(0, 2 * count), :], near), (m_in, mixed), (l_in, logs))
    loads = [copy(source, target, sems.at[slot]) for slot, (source, target) in enumerate(places)]
    for moved in loads:
        moved.wait()
    mine = lax.rem(lax.axis_index("seq"), 4)
    for head in range(2):
        keys = near[:, :count, half(head)].reshape(-1, HEAD_DIM)
        values = near[:, count:, half(head)].reshape(-1, HEAD_DIM)
        dims = (count, 4 * count)
        query = mine * count + lax.broadcasted_iota(jnp.int32, dims, 0)
        key = lax.broadcasted_iota(jnp.int32, dims, 1)
        out, log = attend(queries[:, half(head)], keys, values, key <= query)
        log = jnp.broadcast_to(log, out.shape)
        out, log = merge([(mixed[head, :count, :], logs[head, :count, :]), (out, log)])
        spread_rows(off, head, mixed, run)
        spread_rows(off, head, logs, run_logs)
        where = rows_of(off[head, 0], rows, 4)
        run[head, where, :] = out
        run_logs[head, where, :] = log
        gather_rows(off, head, run, mixed)
        gather_rows(off, head, run_logs, logs)
    moves = [copy(mixed, m_out, sems.at[0]), copy(logs, l_out, sems.at[1])]
    for moved in moves:
        moved.wait()


def far_kernel(near, middle, hi, _, back, zs, part, sems):
    seq = lax.axis_index("seq")
    mine, line = lax.rem(seq, 4), lax.div(seq, 4)
    skip = near.shape[1] - part.shape[1]
    copy(middle, zs, sems.at[0]).wait()
    for level, count, at in ((1, 64, 0), (2, 16, 64)):
        place = lax.rem(line, 4) if level == 1 else line
        logs = []
        for head in range(2):
            queries = near[:, skip + at : skip + at + count, half(head)].reshape(-1, HEAD_DIM)
            if level == 1:
                keys = zs[:, :count, half(head)].reshape(-1, HEAD_DIM)
                values = zs[:, count:, half(head)].reshape(-1, HEAD_DIM)
            else:
                keys = hi[:, :, :count, half(head)].reshape(-1, HEAD_DIM)
                values = hi[:, :, count:, half(head)].reshape(-1, HEAD_DIM)
            dims = (4 * count, keys.shape[0])
            row = lax.broadcasted_iota(jnp.int32, dims, 0)
            query = place * 4 * count + row
            key = lax.broadcasted_iota(jnp.int32, dims, 1)
            key = (lax.div(key, count) * 4 + mine) * count + lax.rem(key, count)
            out, log = attend(queries, keys, values, key <= query)
            logs.append(log)
            part[:, at : at + count, half(head)] = out.reshape(4, count, HEAD_DIM).astype(BF16)
        lane = lax.broadcasted_iota(jnp.int32, (4 * count, HEAD_DIM), 1)
        left = jnp.where(lane < HEAD_DIM // 2, logs[0], logs[1])
        both = left.astype(BF16)
        for piece in range(1, 3):
            left = left - left.astype(BF16).astype(F32)
            both = jnp.where(lax.rem(lane, HEAD_DIM // 2) < 16 * piece, both, left.astype(BF16))
        part[:, at : at + count, 2 * HEAD_DIM :] = both.reshape(4, count, HEAD_DIM)
    moves = [copy(part, back, sems.at[1])]
    for moved in moves:
        moved.wait()


def merge_kernel(off, mixed, logs, back, late, run, run_logs, pack, sems):
    rows = run.shape[1]
    for head in range(2):
        spread_rows(off, head, mixed, run)
        spread_rows(off, head, logs, run_logs)
        at = 0
        for level in (1, 2):
            count = rows // STEPS[level]
            where = rows_of(off[head, level], rows, STEPS[level])
            parts = [(run[head, where, :], run_logs[head, where, :])]
            for source in range(4):
                lane = head * (HEAD_DIM // 2)
                pieces = back[source, at : at + count, 2 * HEAD_DIM :].astype(F32)
                log = sum(pieces[:, lane + 16 * piece : lane + 16 * piece + 1] for piece in range(3))
                value = back[source, at : at + count, half(head)].astype(F32)
                parts.append((value, jnp.broadcast_to(log, (count, HEAD_DIM))))
            at += count
            out, log = merge(parts)
            run[head, where, :] = out
            run_logs[head, where, :] = log
        at = 0
        for level, step in enumerate(STEPS):
            count = rows // step
            pack[at : at + count, half(head)] = run[head, rows_of(off[head, level], rows, step), :].astype(BF16)
            at += count
    moves = [copy(pack, late.at[target], sems.at[target]) for target in range(4)]
    for moved in moves:
        moved.wait()


def project_kernel(marks, own, e1, e2, e3, late, w, send, whole, e0, wide, weight, sems):
    rows, width = send.shape
    part = rows // 4
    most = 3 * part
    place = lax.axis_index("head")
    chip, core = lax.div(place, 2), lax.rem(place, 2)
    column = pl.multiple_of(2 * chip * width, width)
    loads = [
        copy(own.at[pl.ds(0, most), :], e0, sems.at[0]),
        copy(w.at[:, pl.ds(column, 2 * width)], weight, sems.at[1]),
    ]
    for shift, pack in ((1, e1), (2, e2), (3, e3), (0, e0)):
        group = lax.rem(chip + 4 - shift, 4)
        if shift == 0:
            for moved in loads:
                moved.wait()
        for head in range(2):
            slot = 2 * shift + head
            first = marks[shift, 0, head]
            for turn in range(3):
                block = pl.multiple_of(lax.rem(first + turn + 1, 4) * part, part)
                whole[pl.ds(block, part), half(slot)] = pack[turn * part : (turn + 1) * part, half(head)]
            whole[pl.ds(pl.multiple_of(first * part, part), part), half(slot)] = late[group, :part, half(head)]
            at = part
            for level in (1, 2):
                step = STEPS[level] // 4
                count = part // step
                mark = marks[shift, level, head]
                block = pl.multiple_of(lax.rem(mark, 4) * part, part)
                held = 2 * slot + level - 1
                wide[held] = whole[pl.ds(block, part), half(slot)].astype(F32)
                wide[held, pl.ds(lax.div(mark, 4), count, stride=step), :] = late[
                    group, at : at + count, half(head)
                ].astype(F32)
                whole[pl.ds(block, part), half(slot)] = wide[held].astype(BF16)
                at += count

    send[...] = product(whole, (e1, e2, e3), weight, 1 - core).astype(BF16)


def product(whole, packs, weight, which):
    rows, width = whole.shape[0], weight.shape[0]
    first = weight[:, pl.ds(pl.multiple_of(which * width, width), width)]
    total = jnp.dot(whole[:, :width], first, preferred_element_type=F32)
    for shift, pack in enumerate(packs, 1):
        chosen = pack[pl.ds(pl.multiple_of(3 * rows // 4 + 16 + which * width, 16), width), :]
        total = total + jnp.dot(whole[:, shift * width : (shift + 1) * width], chosen, preferred_element_type=F32)
    return total


def keep_kernel(whole, e1, e2, e3, w, keep, weight, sem):
    place = lax.axis_index("head")
    chip, core = lax.div(place, 2), lax.rem(place, 2)
    width = weight.shape[0]
    column = pl.multiple_of(2 * chip * width, width)
    copy(w.at[:, pl.ds(column, 2 * width)], weight, sem).wait()
    keep[...] = product(whole, (e1, e2, e3), weight, core)


def finish_kernel(keep, other, out, wide):
    part = keep.shape[0] // 4
    for head in range(2):
        for turn in range(4):
            block = slice(turn * part, (turn + 1) * part)
            wide[head, pl.ds(turn, part, stride=4), :] = keep[block, half(head)] + other[block, half(head)].astype(F32)
        out[:, half(head)] = wide[head].astype(BF16)


def shards(queries, keys, values, offsets, w_out):
    rows, width = queries.shape
    spread, heads = lax.axis_size("seq"), lax.axis_size("head")
    lines = spread // 4
    along_y = [[4 * line + y for y in range(4)] for line in range(lines)]
    far_lines = [[(4 * b + line) * 4 + y for b in range(4)] for line in range(4) for y in range(4)]
    along_x = [[2 * chip + core for chip in range(4)] for core in range(2)]
    dma = pltpu.SemaphoreType.DMA

    def swap(value, axis, groups):
        return lax.all_to_all(value, axis, 0, 0, axis_index_groups=groups)

    def shift_z(value, by):
        hops = [(4 * (4 * b + z) + y, 4 * (4 * b + (z + by) % 4) + y) for b in range(lines // 4) for z in range(4) for y in range(4)]
        return lax.ppermute(value, "seq", hops)

    def shift_x(value, by):
        return lax.ppermute(value, "head", [(place, (place + 2 * by) % heads) for place in range(heads)])

    count = [rows // step for step in STEPS]
    late_rows = sum(count)
    near_rows = 2 * count[0] + count[1] + count[2]
    z_rows = 2 * count[1] + 2 * count[2]
    raw_offsets = offsets
    queries, keys, values, offsets, w_out = map(stay, (queries, keys, values, offsets, w_out))
    near, near_z, own_q = call(
        pick_kernel,
        (pltpu.HBM((4, near_rows, width), BF16), pltpu.HBM((z_rows, width), BF16), pltpu.HBM((count[0], width), BF16)),
        [HBM] * 4,
        (HBM,) * 3,
        [
            pltpu.SMEM((2, 3), jnp.int32),
            pltpu.VMEM((3, rows, width), BF16),
            pltpu.VMEM((3, 2, rows, HEAD_DIM), F32),
            pltpu.VMEM((near_rows, width), BF16),
            pltpu.VMEM((z_rows, width), BF16),
            pltpu.VMEM((count[0], width), BF16),
            dma((21,)),
        ],
    )(offsets, queries, keys, values)
    zs = [near_z] + [shift_z(near_z, by) for by in (1, 2, 3)]
    near = swap(near, "seq", along_y)
    most = 3 * rows // 4
    packed = pltpu.HBM((most + 16 + 2 * width, width), BF16)
    kept = pltpu.HBM((2, late_rows, HEAD_DIM), F32)
    early, *packs, mixed, logs = call(
        local_kernel,
        (pltpu.HBM((most + 16, width), BF16), packed, packed, packed, kept, kept),
        [HBM] * 5,
        (HBM,) * 6,
        [
            pltpu.SMEM((2, 3), jnp.int32),
            pltpu.VMEM((2, 3, rows, HEAD_DIM), BF16),
            pltpu.VMEM((2, 2, rows, HEAD_DIM), F32),
            pltpu.VMEM((most + 16, width), BF16),
            pltpu.VMEM((2, late_rows, HEAD_DIM), F32),
            pltpu.VMEM((2, late_rows, HEAD_DIM), F32),
            pltpu.VMEM(w_out.shape, BF16),
            dma((26,)),
        ],
    )(offsets, queries, keys, values, w_out)
    far_z, middle = call(
        relay_kernel,
        (pltpu.HBM((4, 4, 2 * count[2], width), BF16), pltpu.HBM((4, 2 * count[1], width), BF16)),
        [VMEM] * 4 + [HBM, ANY],
        (HBM,) * 2,
        [pltpu.VMEM((4, 2 * count[2], width), BF16), dma((8,))],
    )(*zs, stay(early), near)
    far_z = swap(far_z, "seq", far_lines)
    packs = [shift_x(pack, by) for by, pack in enumerate(packs, 1)]
    marks = jnp.stack([part[most : most + 3, ::HEAD_DIM] for part in [early] + packs]).astype(jnp.int32)
    mixed, logs = call(
        near_kernel,
        (kept, kept),
        [HBM] * 2 + [ANY] + [HBM] * 2,
        (HBM,) * 2,
        [
            pltpu.SMEM((2, 3), jnp.int32),
            pltpu.VMEM((count[0], width), BF16),
            pltpu.VMEM((4, 2 * count[0], width), BF16),
            pltpu.VMEM(mixed.shape, F32),
            pltpu.VMEM(mixed.shape, F32),
            pltpu.VMEM((2, rows, HEAD_DIM), F32),
            pltpu.VMEM((2, rows, HEAD_DIM), F32),
            dma((5,)),
        ],
    )(offsets, stay(own_q), near, stay(mixed), stay(logs))
    back = call(
        far_kernel,
        pltpu.HBM((4, count[1] + count[2], 3 * HEAD_DIM), BF16),
        [VMEM, HBM, VMEM, HBM],
        HBM,
        [
            pltpu.VMEM((4, 2 * count[1], width), BF16),
            pltpu.VMEM((4, count[1] + count[2], 3 * HEAD_DIM), BF16),
            dma((2,)),
        ],
    )(near, stay(middle), far_z, stay(mixed))
    back = swap(back, "seq", along_y)
    late = call(
        merge_kernel,
        pltpu.HBM((4, late_rows, width), BF16),
        [SMEM] + [VMEM] * 3,
        HBM,
        [
            pltpu.VMEM((2, rows, HEAD_DIM), F32),
            pltpu.VMEM((2, rows, HEAD_DIM), F32),
            pltpu.VMEM((late_rows, width), BF16),
            dma((4,)),
        ],
    )(raw_offsets, mixed, logs, back)
    late = swap(late, "head", along_x)
    send, whole = call(
        project_kernel,
        (shape((rows, width), BF16), shape((rows, 4 * width), BF16)),
        [SMEM, HBM] + [VMEM] * 4 + [HBM],
        (VMEM,) * 2,
        [
            pltpu.VMEM((most, width), BF16),
            pltpu.VMEM((16, count[0], HEAD_DIM), F32),
            pltpu.VMEM((width, 2 * width), BF16),
            dma((2,)),
        ],
    )(marks, stay(early), *packs, late, w_out)
    keep = call(
        keep_kernel,
        shape((rows, width), F32),
        [VMEM] * 4 + [HBM],
        VMEM,
        [pltpu.VMEM((width, 2 * width), BF16), dma(())],
    )(whole, *packs, w_out)
    other = lax.ppermute(send, "head", [(place, place ^ 1) for place in range(heads)])
    return call(
        finish_kernel,
        shape((rows, width), BF16),
        [VMEM] * 2,
        VMEM,
        [pltpu.VMEM((2, rows, HEAD_DIM), F32)],
    )(keep, other)


def solution(mesh):
    in_specs = (
        P("seq", "head"),
        P("seq", "head"),
        P("seq", "head"),
        P("head", None),
        P("head", None),
    )
    out_specs = P("seq", "head")
    return jax.shard_map(shards, mesh=mesh, in_specs=in_specs, out_specs=out_specs, check_vma=False)
```
